512 devices in a mesh: dp: 32 (over z, core), member: 16 (over y, x).
Axes of the slice: x: 4, y: 4, z: 16, core: 2. Of those that a mesh axis runs over, the one named last changes fastest.
Arguments:
- tokens: bfloat16 [4096, 4096], P('dp', 'member'), may hold values from -6 to 6
- routes: int32 [4096, 2], P('dp'), may hold values from 0 to 7, all different within a row; in each aligned block of 128 rows (0 to 127, 128 to 255, ...) at most 34 rows name the same one
- route_weights: float32 [4096, 2], P('dp'), may hold values from 0.2 to 1
- up_stacked: bfloat16 [8, 4096, 7168], P(None, ('member', 'dp')), may hold values from -0.09375 to 0.09375
- down_stacked: bfloat16 [8, 4096, 7168], P(None, ('member', 'dp')), may hold values from -0.0625 to 0.0625
- cotangent: bfloat16 [4096, 4096], P('dp', 'member'), may hold values from -6 to 6
Outputs:
- mixed: bfloat16 [4096, 4096], P('dp', 'member')
- grad_tokens: bfloat16 [4096, 4096], P('dp', 'member')
- grad_up: bfloat16 [32, 4096, 1792], P('dp', 'member')
- grad_down: bfloat16 [32, 4096, 1792], P('dp', 'member')
The draws below stay inside these ranges and needn't reach their ends.
Inputs may be any that keep to these rules, and one draw needn't show every extreme that they name: `routes`: each row names two different experts. In each aligned block of 128 rows no expert is named by more than 34 rows, and in some block some expert is named by exactly 34 rows.
All inputs are finite; a program needn't handle non-finite values.
Results may differ from the reference program's by a relative error of at most 0.018.
Values may be sent and summed in bfloat16 or wider, within the bound.
A program may use at most 64 MiB of HBM per device.

```python
import math
import jax
import jax.numpy as jnp
import numpy as np
from jax import lax

D = 4096
FF_W = 7168
E = 8
TOK_DEV = 128
CAP = 34
TOKENS = 4096
N_DP = 32
N_MEMBER = 16


def block_levels(rng, extent, cuts, low, largest):
    def one(position, parts):
        draws = jax.random.uniform(jax.random.fold_in(jax.random.fold_in(rng, 6), position), (parts,), jnp.float32, low / len(cuts), largest / len(cuts))
        return jnp.repeat(jnp.exp(draws), extent[position] // parts).reshape((-1,) + (1,) * (len(extent) - position - 1))

    factor_of = one(*cuts[0])
    for cut in cuts[1:]:
        factor_of = factor_of * one(*cut)
    return factor_of


def deal_out(stream_key, own, number, rows, count, top, limit, slope):
    sequence = jax.random.permutation(stream_key, count)
    heavy_load, common = portions_of(count, rows * top, limit, slope, True), portions_of(count, rows * top, limit, slope, False)
    places = jnp.arange(count)

    def named(sizes, rotation):
        used = int((sizes > 0).sum())
        fixed = max(1, used // 4)
        moved = fixed + (places - fixed + rotation * (used - fixed)) % max(1, count - fixed)
        return jnp.zeros((count,), jnp.int32).at[sequence[jnp.where(places < fixed, places, moved)]].set(jnp.asarray(sizes, jnp.int32))

    sizes = jnp.where(number % 4 == 0, named(heavy_load, number // 4), named(common, number - number // 4 - 1))
    mixed = jax.random.permutation(jax.random.fold_in(own, 3), count)
    donor, taker = mixed[0:count // 2 * 2:2], mixed[1:count // 2 * 2:2]
    room = jnp.minimum(sizes[donor] - 1, limit - sizes[taker]) // 2
    room = jnp.where((donor == sequence[0]) | (taker == sequence[0]) | (sizes[taker] == 0), 0, jnp.maximum(room, 0))
    moved = jax.random.randint(jax.random.fold_in(own, 4), (count // 2,), 0, 1 << 20) % (room + 1)
    sizes = sizes.at[donor].add(-moved).at[taker].add(moved)
    labels = jnp.searchsorted(jnp.cumsum(sizes), jnp.arange(rows * top), side="right").astype(jnp.int32)
    listing = labels.reshape(top, rows).T
    listing = listing[jax.random.permutation(jax.random.fold_in(own, 1), rows)]
    rotation = jax.random.randint(jax.random.fold_in(own, 2), (rows, 1), 0, top)
    return jnp.take_along_axis(listing, (jnp.arange(top)[None, :] + rotation) % top, axis=1)


def portions_of(count, total, bound, skew, full):
    weights = [(1 << 20) // math.isqrt(grade ** skew) + 1 for grade in range(1, count + 1)]
    largest = bound if full else min(bound, max(-(-total // count), total * weights[0] // sum(weights)))
    least = 1 if total - largest >= count - 1 else 0
    holding, spare = [largest] + [least] * (count - 1), total - largest - least * (count - 1)
    while spare > 0:
        candidates = [i for i in range(1, count) if holding[i] < largest] or [i for i in range(1, count) if holding[i] < bound]
        pool, left = sum([weights[i] for i in candidates]), spare
        for i in candidates:
            more = min(bound - holding[i], max(1, left * weights[i] // pool), spare)
            holding[i] = holding[i] + more
            spare = spare - more
    return np.array(holding)


def scatter_about(key, shape, deviation, reach, split=(), kind=jnp.bfloat16):
    level = block_levels(key, shape, split, -0.22, 0.18) if split else 1.0
    entries = jax.random.normal(key, shape, jnp.float32) * deviation * level
    return jnp.minimum(jnp.maximum(entries, -reach), reach).astype(kind)


def setup_inputs(seed: int = 0) -> dict:
    seeds = jax.random.split(jax.random.key(seed), 7)
    tokens = scatter_about(seeds[0], (TOKENS, D), 1.0, 6.0, ((0, 32), (1, 16)))
    routes_keys = jax.random.split(jax.random.fold_in(seeds[1], 1), TOKENS // TOK_DEV)
    routes_turns = jax.random.permutation(jax.random.fold_in(seeds[1], 3), TOKENS // TOK_DEV)
    routes = jax.vmap(lambda own, number: deal_out(jax.random.fold_in(seeds[1], 2), own, number, TOK_DEV, E, 2, CAP, 2))(routes_keys, routes_turns).reshape((TOKENS, 2))
    route_weights = jnp.clip(0.2 + 0.8 * jax.random.uniform(seeds[2], (TOKENS, 2), jnp.float32) ** block_levels(seeds[2], (TOKENS, 2), ((0, 32),), -0.2, 0.2), 0.2, 1.0)
    up_stacked = scatter_about(seeds[3], (E, D, FF_W), D ** -0.5, 0.09375, ((1, 512),))
    down_stacked = scatter_about(seeds[4], (E, D, FF_W), FF_W ** -0.5, 0.0625, ((1, 512),))
    cotangent = scatter_about(seeds[5], (TOKENS, D), 1.0, 6.0, ((0, 32), (1, 16)))
    return dict(tokens=tokens, routes=routes, route_weights=route_weights, up_stacked=up_stacked, down_stacked=down_stacked, cotangent=cotangent)


def group_sum(left, right):
    row_total = left.shape[0]
    left_groups = left.astype(jnp.float32).reshape(row_total, N_MEMBER, -1)
    right_groups = right.astype(jnp.float32).reshape(N_MEMBER, -1, right.shape[1])
    partial_value = jnp.einsum("rgd,gdf->grf", left_groups, right_groups)
    rounded = lax.optimization_barrier(partial_value.astype(jnp.bfloat16))
    return jnp.sum(rounded.astype(jnp.float32), axis=0)


def owner_layout(full, quarters, hidden_own):
    return full.reshape(E, D, quarters, hidden_own).transpose(0, 2, 1, 3).reshape(E * quarters, D, hidden_own)


def reference(tokens, routes, route_weights, up_stacked, down_stacked, cotangent):
    quarters = N_DP // E
    hidden_own = FF_W // quarters
    token_total = tokens.shape[0]
    chosen = (routes[:, :, None] == jnp.arange(E, dtype=jnp.int32)[None, None, :]).astype(jnp.int32)
    blocked = chosen.reshape(N_DP, TOK_DEV * 2, E)
    before = jnp.cumsum(blocked, axis=1) - blocked
    slot_pos = jnp.sum(before * blocked, axis=2).reshape(token_total, 2).astype(jnp.int32)
    source = (jnp.arange(token_total, dtype=jnp.int32) // TOK_DEV).astype(jnp.int32)
    row_index = (source[:, None] * CAP + slot_pos).astype(jnp.int32)
    flat_index = (routes * (N_DP * CAP) + row_index).astype(jnp.int32)
    owner = jnp.full((E * N_DP * CAP,), -1, jnp.int32)
    owner = owner.at[flat_index.reshape(-1)].set(jnp.arange(token_total * 2, dtype=jnp.int32))
    owner = owner.reshape(E, N_DP * CAP)
    filled = owner >= 0
    safe_owner = jnp.maximum(owner, 0)
    token_of = safe_owner // 2
    weight_of = jnp.where(filled, route_weights.reshape(-1)[safe_owner], jnp.zeros((), jnp.float32))
    x_slots = jnp.where(filled[:, :, None], tokens[token_of], jnp.zeros((), tokens.dtype))
    d_slots = (weight_of[:, :, None] * cotangent[token_of].astype(jnp.float32)).astype(jnp.bfloat16)

    def expert(inputs):
        x_rows, d_rows, up_w, down_w = inputs
        pre = group_sum(x_rows, up_w)
        act = jax.nn.silu(pre).astype(jnp.bfloat16)
        y_rows = jnp.dot(act, down_w.T, preferred_element_type=jnp.float32)
        d_act = group_sum(d_rows, down_w)
        sig = jax.nn.sigmoid(pre)
        d_pre = (d_act * sig * (1.0 + pre * (1.0 - sig))).astype(jnp.bfloat16)
        g_down = jnp.dot(d_rows.T, act, preferred_element_type=jnp.float32).astype(jnp.bfloat16)
        g_up = jnp.dot(x_rows.T, d_pre, preferred_element_type=jnp.float32).astype(jnp.bfloat16)
        dx_rows = jnp.dot(d_pre, up_w.T, preferred_element_type=jnp.float32)
        return y_rows, dx_rows, g_up, g_down

    y_all, dx_all, g_up, g_down = lax.map(expert, (x_slots, d_slots, up_stacked, down_stacked))
    y_pick = y_all[routes, row_index]
    mixed = (route_weights[:, 0, None] * y_pick[:, 0] + route_weights[:, 1, None] * y_pick[:, 1]).astype(jnp.bfloat16)
    dx_pick = dx_all[routes, row_index]
    grad_tokens = (dx_pick[:, 0] + dx_pick[:, 1]).astype(jnp.bfloat16)
    return mixed, grad_tokens, owner_layout(g_up, quarters, hidden_own), owner_layout(g_down, quarters, hidden_own)
```

```python
import jax
import jax.numpy as jnp
from jax import lax
from jax.sharding import PartitionSpec as P

FF_W = 7168
E = 8
CAP = 34


def contract(left, right, left_dim, right_dim):
    return lax.dot_general(
        left, right, (((left_dim,), (right_dim,)), ((), ())), preferred_element_type=jnp.float32
    )


def body(tokens, routes, route_weights, up_stacked, down_stacked, cotangent):
    dp_count = lax.axis_size("dp")
    member_count = lax.axis_size("member")
    quarters = dp_count // E
    share_rows = up_stacked.shape[1]
    features = tokens.shape[1]
    hidden_own = FF_W // quarters
    per_member = hidden_own // member_count
    slots_all = E * CAP
    up_parts = (
        up_stacked.reshape(E, share_rows, quarters, hidden_own)
        .transpose(0, 2, 1, 3)
        .reshape(dp_count, share_rows, hidden_own)
    )
    down_parts = (
        down_stacked.reshape(E, share_rows, quarters, hidden_own)
        .transpose(0, 2, 1, 3)
        .reshape(dp_count, share_rows, hidden_own)
    )
    up_own, down_own = (
        lax.all_to_all(up_parts, "dp", split_axis=0, concat_axis=1, tiled=True),
        lax.all_to_all(down_parts, "dp", split_axis=0, concat_axis=1, tiled=True),
    )
    up_own = up_own.reshape(dp_count * share_rows, hidden_own)
    down_own = down_own.reshape(dp_count * share_rows, hidden_own)
    chosen = jnp.sum(
        (routes[:, :, None] == jnp.arange(E, dtype=jnp.int32)[None, None, :]).astype(jnp.float32),
        axis=1,
    )
    rows = jnp.arange(routes.shape[0], dtype=jnp.int32)
    earlier = (rows[None, :] < rows[:, None]).astype(jnp.bfloat16)
    before = jnp.dot(
        earlier, chosen.astype(jnp.bfloat16), preferred_element_type=jnp.float32
    ).astype(jnp.int32)
    slot_pos = jnp.sum(
        jnp.where(
            routes[:, :, None] == jnp.arange(E, dtype=jnp.int32)[None, None, :],
            before[:, None, :],
            0,
        ),
        axis=2,
    )
    target = routes * CAP + slot_pos
    slot_hits = jnp.arange(slots_all, dtype=jnp.int32)[:, None, None] == target[None, :, :]
    pick_table = jnp.sum(slot_hits.astype(jnp.float32), axis=2)
    weighted = jnp.sum(jnp.where(slot_hits, route_weights[None, :, :], 0.0), axis=2)
    x_local = jnp.dot(
        pick_table.astype(jnp.bfloat16), tokens, preferred_element_type=jnp.float32
    ).astype(jnp.bfloat16)
    d_local = jnp.dot(
        weighted, cotangent.astype(jnp.float32), precision=lax.Precision.HIGHEST
    ).astype(jnp.bfloat16)

    def spread(local):
        return jnp.broadcast_to(
            local.reshape(E, 1, CAP, features), (E, quarters, CAP, features)
        ).reshape(dp_count, CAP, features)

    def collect(returned):
        return jnp.sum(returned.reshape(E, quarters, CAP, features), axis=1).reshape(
            slots_all, features
        )

    x_in = lax.all_to_all(spread(x_local), "dp", split_axis=0, concat_axis=0, tiled=True).reshape(
        dp_count * CAP, features
    )
    partial_value = jnp.dot(x_in, up_own, preferred_element_type=jnp.float32).astype(jnp.bfloat16)
    pre_full = lax.psum(partial_value, "member").astype(jnp.float32)
    act_full = jax.nn.silu(pre_full).astype(jnp.bfloat16)
    y_part = contract(act_full, down_own, 1, 1)
    y_part, pre_full, act_full = (y_part, pre_full, act_full)
    y_back = lax.all_to_all(
        y_part.reshape(dp_count, CAP, features).astype(jnp.bfloat16),
        "dp",
        split_axis=0,
        concat_axis=0,
        tiled=True,
    ).astype(jnp.float32)
    d_in = lax.all_to_all(spread(d_local), "dp", split_axis=0, concat_axis=0, tiled=True).reshape(
        dp_count * CAP, features
    )
    d_act = lax.psum_scatter(
        contract(down_own, d_in, 0, 1).astype(jnp.bfloat16),
        "member",
        scatter_dimension=0,
        tiled=True,
    ).astype(jnp.float32)
    own_start = lax.axis_index("member") * per_member
    pre_share = lax.dynamic_slice_in_dim(pre_full, own_start, per_member, 1).T
    sigma = jax.nn.sigmoid(pre_share)
    d_share = (d_act * sigma * (1.0 + pre_share * (1.0 - sigma))).astype(jnp.bfloat16)
    d_pre = lax.all_gather(d_share, "member", axis=0, tiled=True)
    g_down = contract(d_in, act_full, 0, 0)
    g_up = contract(x_in, d_pre, 0, 1)
    dx_part = contract(d_pre, up_own, 0, 1)
    dx_part, g_up, g_down = (dx_part, g_up, g_down)
    dx_back = lax.all_to_all(
        dx_part.reshape(dp_count, CAP, features).astype(jnp.bfloat16),
        "dp",
        split_axis=0,
        concat_axis=0,
        tiled=True,
    ).astype(jnp.float32)
    y_slots = collect(y_back)
    dx_slots = collect(dx_back)
    mixed = jnp.dot(weighted.T, y_slots, precision=lax.Precision.HIGHEST).astype(jnp.bfloat16)
    grad_tokens = jnp.dot(pick_table.T, dx_slots, precision=lax.Precision.HIGHEST).astype(
        jnp.bfloat16
    )
    grad_up = g_up.astype(jnp.bfloat16).reshape(1, features, hidden_own)
    grad_down = g_down.astype(jnp.bfloat16).reshape(1, features, hidden_own)
    return (mixed, grad_tokens, grad_up, grad_down)


def solution(mesh):
    placed = (
        P("dp", "member"),
        P("dp", None),
        P("dp", None),
        P(None, ("member", "dp"), None),
        P(None, ("member", "dp"), None),
        P("dp", "member"),
    )
    return jax.shard_map(
        body,
        mesh=mesh,
        in_specs=placed,
        out_specs=(
            P("dp", "member"),
            P("dp", "member"),
            P("dp", "member", None),
            P("dp", "member", None),
        ),
        check_vma=False,
    )
```

```python
import jax
import jax.numpy as jnp
from jax import lax
from jax.experimental import pallas as pl
from jax.experimental.pallas import tpu as pltpu
from jax.sharding import PartitionSpec as P

FF_W = 7168
E = 8
CAP = 34
SIDE = 4
HEAD = 32
TAIL = 8
MSG = HEAD + TAIL
BF = jnp.bfloat16
F32 = jnp.float32


def dot(a, b, ca, cb):
    return lax.dot_general(a, b, (((ca,), (cb,)), ((), ())), preferred_element_type=F32)


def mult(i, n):
    return pl.multiple_of(i, n)


def layer_kernel(
    x_msg, d_msg, up, down,
    y_out, dx_out, gu_out, gd_out,
    up_own, down_own, x_got, d_got, y_msg, y_got, dx_msg, dx_got,
    xm, xt, dm, dt, tail32,
    pm, pt, r1m, r1t, sm, st, r2m, r2t, pre_m, pre_t, fm, ft,
    z_send, z_recv, o_send, o_recv, rs_send, rs_recv, ag_send, ag_recv,
):
    n_dp = lax.axis_size("dp")
    quarters = n_dp // E
    hid = up_own.shape[2]
    own_f = xm.shape[1]
    j = lax.axis_index("dp")
    m = lax.axis_index("member")
    cy, cx = m // SIDE, lax.rem(m, SIDE)
    half_rows = n_dp * HEAD // 2
    big = half_rows // SIDE
    small = big // SIDE
    t_rows = n_dp // 4 * TAIL
    ht = t_rows // 2
    wide = pt.shape[2] // SIDE
    narrow = wide // SIDE

    def first(h):
        return cx if h == 0 else cy

    def second(h):
        return cy if h == 0 else cx

    def peer_first(h, k):
        c = lax.rem(first(h) + k, SIDE)
        return c, {"member": cy * SIDE + c if h == 0 else c * SIDE + cx}

    def peer_second(h, k):
        c = lax.rem(second(h) + k, SIDE)
        return c, {"member": c * SIDE + cx if h == 0 else cy * SIDE + c}

    def shifted(i):
        step = i // 2 + 1
        return lax.rem(j + n_dp + step * (1 - 2 * lax.rem(i, 2)), n_dp)

    barrier = pltpu.get_barrier_semaphore()

    @pl.loop(0, n_dp - 1)
    def _(i):
        pl.semaphore_signal(barrier, inc=1, device_id={"dp": shifted(i)})

    for k in range(1, SIDE):
        pl.semaphore_signal(barrier, inc=1, device_id=peer_first(0, k)[1])
        pl.semaphore_signal(barrier, inc=1, device_id=peer_first(1, k)[1])
    pl.semaphore_wait(barrier, n_dp - 1 + 2 * (SIDE - 1))

    def weight_part(w, who):
        return w.at[who // quarters, :, pl.ds(mult(lax.rem(who, quarters) * hid, 128), hid)]

    def dispatch(n, msg, got, w, own):
        @pl.loop(0, n_dp - 1)
        def _(i):
            who = shifted(i)
            pltpu.make_async_remote_copy(
                src_ref=msg.at[who // quarters], dst_ref=got.at[j],
                send_sem=z_send.at[2 * n], recv_sem=z_recv.at[2 * n], device_id={"dp": who},
            ).start()

        pltpu.make_async_copy(msg.at[j // quarters], got.at[j], z_recv.at[2 * n]).start()

        @pl.loop(0, n_dp - 1)
        def _(i):
            who = shifted(i)
            pltpu.make_async_remote_copy(
                src_ref=weight_part(w, who), dst_ref=own.at[j],
                send_sem=z_send.at[2 * n + 1], recv_sem=z_recv.at[2 * n + 1], device_id={"dp": who},
            ).start()

        pltpu.make_async_copy(weight_part(w, j), own.at[j], z_recv.at[2 * n + 1]).start()

    def take(buf, sem):
        pltpu.make_async_copy(buf, buf, sem).wait()

    def sent(buf, sem):
        part = buf.at[pl.ds(0, n_dp - 1)]
        pltpu.make_async_copy(part, part, sem).wait()

    def gather_rows(got, main, tail):
        @pl.loop(0, n_dp)
        def _(s):
            main[pl.ds(mult(s * HEAD, HEAD), HEAD), :] = got[s, :HEAD, :]

        @pl.loop(0, n_dp // 4)
        def _(g):
            total = got[4 * g, HEAD:, :].astype(F32)
            for i in range(1, 4):
                total = total + got[4 * g + i, HEAD:, :].astype(F32)
            tail32[pl.ds(mult(g * TAIL, TAIL), TAIL), :] = total

        tail[...] = tail32[...].astype(BF)

    def partial(t, main, tail, own):
        @pl.loop(0, hid // 256)
        def _(c):
            cols = pl.ds(mult(c * 256, 256), 256)
            w = own[:, :, cols].reshape(own_f, 256)
            pm[t, :, cols] = dot(main[...], w, 1, 0).astype(BF)
            pt[t, :, cols] = dot(tail[...], w, 1, 0).astype(BF)

    def rs_copies(t, stage):
        out = []
        for h in range(2):
            for k in range(1, SIDE):
                if stage == 0:
                    c, dev = peer_first(h, k)
                    pairs = (
                        (pm.at[t, pl.ds(mult(h * half_rows + c * big, big), big), :], r1m.at[t, h, k - 1]),
                        (pt.at[t, pl.ds(h * ht, ht), pl.ds(mult(c * wide, wide), wide)], r1t.at[t, h, k - 1]),
                    )
                else:
                    c, dev = peer_second(h, k)
                    pairs = (
                        (sm.at[t, h, pl.ds(mult(c * small, small), small), :], r2m.at[t, h, k - 1]),
                        (st.at[t, h, :, pl.ds(mult(c * narrow, narrow), narrow)], r2t.at[t, h, k - 1]),
                    )
                for n, (src, dst) in enumerate(pairs):
                    out.append(
                        pltpu.make_async_remote_copy(
                            src_ref=src, dst_ref=dst,
                            send_sem=rs_send.at[t, stage, h, k - 1, n],
                            recv_sem=rs_recv.at[t, stage, h, k - 1, n], device_id=dev,
                        )
                    )
        return out

    def start(copies):
        for c in copies:
            c.start()
        return copies

    def arrived(copies):
        for c in copies:
            c.wait_recv()

    def left(copies):
        for c in copies:
            c.wait_send()

    def sum_first(t):
        for h in range(2):
            base = h * half_rows + first(h) * big

            @pl.loop(0, big // 16)
            def _(i):
                rows = pl.ds(mult(i * 16, 16), 16)
                total = pm[t, pl.ds(mult(base + i * 16, 16), 16), :].astype(F32)
                for k in range(SIDE - 1):
                    total = total + r1m[t, h, k, rows, :].astype(F32)
                sm[t, h, rows, :] = total.astype(BF)

            total = pt[t, pl.ds(h * ht, ht), pl.ds(mult(first(h) * wide, wide), wide)].astype(F32)
            for k in range(SIDE - 1):
                total = total + r1t[t, h, k].astype(F32)
            st[t, h] = total.astype(BF)

    def owned_rows(h):
        return pl.ds(mult(h * half_rows + first(h) * big + second(h) * small, small), small)

    def owned_cols(h):
        return pl.ds(mult(first(h) * wide + second(h) * narrow, narrow), narrow)

    def finish(t, fn):
        for h in range(2):

            @pl.loop(0, small // 16)
            def _(i):
                rows = pl.ds(mult(i * 16, 16), 16)
                total = sm[t, h, pl.ds(mult(second(h) * small + i * 16, 16), 16), :].astype(F32)
                for k in range(SIDE - 1):
                    total = total + r2m[t, h, k, rows, :].astype(F32)
                start_row = h * half_rows + first(h) * big + second(h) * small
                fm[t, pl.ds(mult(start_row + i * 16, 16), 16), :] = fn(total, pre_m.at[h, rows, :]).astype(BF)

            total = st[t, h, :, pl.ds(mult(second(h) * narrow, narrow), narrow)].astype(F32)
            for k in range(SIDE - 1):
                total = total + r2t[t, h, k].astype(F32)
            ft[t, pl.ds(h * ht, ht), owned_cols(h)] = fn(total, pre_t.at[h]).astype(BF)

    def silu(total, keep):
        keep[...] = total
        return total / (1.0 + jnp.exp(-total))

    def silu_back(total, keep):
        pre = keep[...]
        s = 1.0 / (1.0 + jnp.exp(-pre))
        return total * s * (1.0 + pre * (1.0 - s))

    def ag_copies(t, stage):
        out = []
        for h in range(2):
            if stage == 0:
                rows, cols = owned_rows(h), owned_cols(h)
            else:
                rows = pl.ds(mult(h * half_rows + first(h) * big, big), big)
                cols = pl.ds(mult(first(h) * wide, wide), wide)
            for k in range(1, SIDE):
                dev = (peer_second if stage == 0 else peer_first)(h, k)[1]
                for n, ref in enumerate((fm.at[t, rows, :], ft.at[t, pl.ds(h * ht, ht), cols])):
                    out.append(
                        pltpu.make_async_remote_copy(
                            src_ref=ref, dst_ref=ref,
                            send_sem=ag_send.at[t, stage, h, k - 1, n],
                            recv_sem=ag_recv.at[t, stage, h, k - 1, n], device_id=dev,
                        )
                    )
        return out

    def back(t, own, msg):
        flat = own[...].reshape(own_f, hid)

        @pl.loop(0, n_dp // 8)
        def _(b):
            part = dot(fm[t, pl.ds(mult(b * 8 * HEAD, 8 * HEAD), 8 * HEAD), :], flat, 1, 1).astype(BF)
            for i in range(8):
                msg[8 * b + i, :HEAD, :] = part[i * HEAD : (i + 1) * HEAD, :]

        tail32[...] = dot(ft[t, :, :hid], flat, 1, 1)

        @pl.loop(0, n_dp)
        def _(s):
            msg[s, HEAD:, :] = tail32[pl.ds(mult(s // 4 * TAIL, TAIL), TAIL), :].astype(BF)

    def give_back(t, msg, got):
        @pl.loop(0, n_dp - 1)
        def _(i):
            who = shifted(i)
            pltpu.make_async_remote_copy(
                src_ref=msg.at[who], dst_ref=got.at[j],
                send_sem=o_send.at[t], recv_sem=o_recv.at[t], device_id={"dp": who},
            ).start()

        pltpu.make_async_copy(msg.at[j], got.at[j], o_recv.at[t]).start()

    def collect(got, out):
        @pl.loop(0, E)
        def _(e):
            total = got[quarters * e].astype(F32)
            for q in range(1, quarters):
                total = total + got[quarters * e + q].astype(F32)
            out[e] = total

    def gradient(main, tail, t, out):
        left_m, left_t = main[...], tail[...]

        @pl.loop(0, hid // 256)
        def _(c):
            cols = pl.ds(mult(c * 256, 256), 256)
            g = dot(left_m, fm[t, :, cols], 0, 0) + dot(left_t, ft[t, :, cols], 0, 0)
            out[:, cols] = g.astype(BF)

    dispatch(0, x_msg, x_got, up, up_own)
    dispatch(1, d_msg, d_got, down, down_own)
    pt[:, :, hid:] = jnp.zeros((2, t_rows, pt.shape[2] - hid), BF)

    take(x_got, z_recv.at[0])
    gather_rows(x_got, xm, xt)
    take(up_own, z_recv.at[1])
    partial(0, xm, xt, up_own)
    rs00 = start(rs_copies(0, 0))
    arrived(rs00)
    sum_first(0)
    rs01 = start(rs_copies(0, 1))
    arrived(rs01)
    finish(0, silu)
    ag00 = start(ag_copies(0, 0))
    arrived(ag00)
    ag01 = start(ag_copies(0, 1))

    take(d_got, z_recv.at[2])
    gather_rows(d_got, dm, dt)
    take(down_own, z_recv.at[3])
    partial(1, dm, dt, down_own)
    rs10 = start(rs_copies(1, 0))
    arrived(ag01)
    back(0, down_own, y_msg)
    give_back(0, y_msg, y_got)
    arrived(rs10)
    sum_first(1)
    rs11 = start(rs_copies(1, 1))
    arrived(rs11)
    finish(1, silu_back)
    ag10 = start(ag_copies(1, 0))
    arrived(ag10)
    ag11 = start(ag_copies(1, 1))
    gradient(dm, dt, 0, gd_out)
    arrived(ag11)
    back(1, up_own, dx_msg)
    give_back(1, dx_msg, dx_got)
    gradient(xm, xt, 1, gu_out)
    take(y_got, o_recv.at[0])
    collect(y_got, y_out)
    take(dx_got, o_recv.at[1])
    collect(dx_got, dx_out)
    for copies in (rs00, rs01, ag00, ag01, rs10, rs11, ag10, ag11):
        left(copies)
    sent(x_got, z_send.at[0])
    sent(up_own, z_send.at[1])
    sent(d_got, z_send.at[2])
    sent(down_own, z_send.at[3])
    sent(y_got, o_send.at[0])
    sent(dx_got, o_send.at[1])


def layer(x_msg, d_msg, up, down):
    n_dp = lax.axis_size("dp")
    own_f = x_msg.shape[2]
    rows = up.shape[1]
    hid = up.shape[2] // (n_dp // E)
    main = n_dp * HEAD
    tails = n_dp // 4 * TAIL
    wide = -(-hid // (SIDE * SIDE * 128)) * SIDE * SIDE * 128
    big = main // 2 // SIDE
    small = big // SIDE
    ht = tails // 2
    vm = pltpu.VMEM
    dma = pltpu.SemaphoreType.DMA
    return pl.pallas_call(
        layer_kernel,
        name="layer",
        out_shape=(
            jax.ShapeDtypeStruct((E, MSG, own_f), F32),
            jax.ShapeDtypeStruct((E, MSG, own_f), F32),
            jax.ShapeDtypeStruct((own_f, hid), BF),
            jax.ShapeDtypeStruct((own_f, hid), BF),
        ),
        in_specs=[pl.BlockSpec(memory_space=pltpu.VMEM)] * 2 + [pl.BlockSpec(memory_space=pl.ANY)] * 2,
        out_specs=[pl.BlockSpec(memory_space=pltpu.VMEM)] * 4,
        scratch_shapes=[
            vm((n_dp, rows, hid), BF), vm((n_dp, rows, hid), BF),
            vm((n_dp, MSG, own_f), BF), vm((n_dp, MSG, own_f), BF),
            vm((n_dp, MSG, own_f), BF), vm((n_dp, MSG, own_f), BF),
            vm((n_dp, MSG, own_f), BF), vm((n_dp, MSG, own_f), BF),
            vm((main, own_f), BF), vm((tails, own_f), BF),
            vm((main, own_f), BF), vm((tails, own_f), BF),
            vm((tails, own_f), F32),
            vm((2, main, hid), BF), vm((2, tails, wide), BF),
            vm((2, 2, SIDE - 1, big, hid), BF), vm((2, 2, SIDE - 1, ht, wide // SIDE), BF),
            vm((2, 2, big, hid), BF), vm((2, 2, ht, wide // SIDE), BF),
            vm((2, 2, SIDE - 1, small, hid), BF), vm((2, 2, SIDE - 1, ht, wide // SIDE // SIDE), BF),
            vm((2, small, hid), F32), vm((2, ht, wide // SIDE // SIDE), F32),
            vm((2, main, hid), BF), vm((2, tails, wide), BF),
            dma((4,)), dma((4,)), dma((2,)), dma((2,)),
            dma((2, 2, 2, SIDE - 1, 2)), dma((2, 2, 2, SIDE - 1, 2)),
            dma((2, 2, 2, SIDE - 1, 2)), dma((2, 2, 2, SIDE - 1, 2)),
        ],
        compiler_params=pltpu.CompilerParams(
            collective_id=0, has_side_effects=True, vmem_limit_bytes=58 * 2**20
        ),
    )(x_msg, d_msg, up, down)


def body(tokens, routes, route_weights, up_stacked, down_stacked, cotangent):
    experts = jnp.arange(E, dtype=jnp.int32)
    named = routes[:, :, None] == experts[None, None, :]
    chosen = jnp.sum(named.astype(F32), axis=1)
    rows = jnp.arange(routes.shape[0], dtype=jnp.int32)
    earlier = (rows[None, :] < rows[:, None]).astype(BF)
    before = jnp.dot(earlier, chosen.astype(BF), preferred_element_type=F32).astype(jnp.int32)
    slot_pos = jnp.sum(jnp.where(named, before[:, None, :], 0), axis=2)
    shift = 2 * lax.rem(lax.axis_index("dp"), 4)
    target = routes * MSG + slot_pos + jnp.where(slot_pos >= HEAD, shift, 0)
    slot_hits = jnp.arange(E * MSG, dtype=jnp.int32)[:, None, None] == target[None, :, :]
    pick_table = jnp.sum(slot_hits.astype(F32), axis=2)
    weighted = jnp.sum(jnp.where(slot_hits, route_weights[None, :, :], 0.0), axis=2)
    features = tokens.shape[1]
    x_msg = jnp.dot(pick_table.astype(BF), tokens, preferred_element_type=F32).astype(BF)
    d_msg = jnp.dot(weighted, cotangent.astype(F32), precision=lax.Precision.HIGHEST).astype(BF)
    y_slots, dx_slots, g_up, g_down = layer(
        x_msg.reshape(E, MSG, features), d_msg.reshape(E, MSG, features), up_stacked, down_stacked
    )
    y_slots = y_slots.reshape(E * MSG, features)
    dx_slots = dx_slots.reshape(E * MSG, features)
    mixed = jnp.dot(weighted.T, y_slots, precision=lax.Precision.HIGHEST).astype(BF)
    grad_tokens = jnp.dot(pick_table.T, dx_slots, precision=lax.Precision.HIGHEST).astype(BF)
    return (mixed, grad_tokens, g_up[None], g_down[None])


def solution(mesh):
    placed = (
        P("dp", "member"),
        P("dp", None),
        P("dp", None),
        P(None, ("member", "dp"), None),
        P(None, ("member", "dp"), None),
        P("dp", "member"),
    )
    return jax.shard_map(
        body,
        mesh=mesh,
        in_specs=placed,
        out_specs=(
            P("dp", "member"),
            P("dp", "member"),
            P("dp", "member", None),
            P("dp", "member", None),
        ),
        check_vma=False,
    )
```

```python
import jax
import jax.numpy as jnp
from jax import lax
from jax.experimental import pallas as pl
from jax.experimental.pallas import tpu as pltpu
from jax.sharding import PartitionSpec as P

FF_W = 7168
E = 8
CAP = 34
SIDE = 4
HEAD = 32
TAIL = 8
MSG = HEAD + TAIL
BF = jnp.bfloat16
F32 = jnp.float32


def dot(a, b, ca, cb):
    return lax.dot_general(a, b, (((ca,), (cb,)), ((), ())), preferred_element_type=F32)


def mult(i, n):
    return pl.multiple_of(i, n)


def layer_kernel(
    x_msg, d_msg, up, down,
    y_out, dx_out, gu_out, gd_out,
    up_own, down_own, x_got, d_got, back_msg, sum_in, sum_far,
    xm, xt, dm, dt, tail32,
    pm, pt, ram, rat, rbm, rbt, sm, st, r2m, r2t, pre_m, pre_t, fm, ft,
    w_send, w_recv, t_send, t_recv, relay_send, relay_recv, fold_send, fold_recv, o_send, o_recv,
    rs_send, rs_recv, rs2_send, rs2_recv, ag_send, ag_recv, ag2_send, ag2_recv,
):
    n_dp = lax.axis_size("dp")
    quarters = n_dp // E
    blocks = n_dp // quarters
    hid = up_own.shape[2]
    own_f = xm.shape[1]
    j = lax.axis_index("dp")
    m = lax.axis_index("member")
    e, q = j // quarters, lax.rem(j, quarters)
    far_q = lax.rem(q + 2, 4)
    near_q = q + 1 - 2 * lax.rem(q, 2)
    near_far_q = lax.rem(near_q + 2, 4)
    cy, cx = m // SIDE, lax.rem(m, SIDE)
    half_rows = n_dp * HEAD // 2
    big = half_rows // SIDE
    small = big // SIDE
    t_rows = blocks * TAIL
    ht = t_rows // 2
    wide = pt.shape[2] // SIDE
    narrow = wide // SIDE
    started = []

    def first(h):
        return cx if h == 0 else cy

    def second(h):
        return cy if h == 0 else cx

    def peer_first(h, k):
        c = lax.rem(first(h) + k, SIDE)
        return c, {"member": cy * SIDE + c if h == 0 else c * SIDE + cx}

    def peer_second(h, k):
        c = lax.rem(second(h) + k, SIDE)
        return c, {"member": c * SIDE + cx if h == 0 else cy * SIDE + c}

    def shifted(i):
        step = i // 2 + 1
        return lax.rem(j + n_dp + step * (1 - 2 * lax.rem(i, 2)), n_dp)

    barrier = pltpu.get_barrier_semaphore()

    @pl.loop(0, n_dp - 1)
    def _(i):
        pl.semaphore_signal(barrier, inc=1, device_id={"dp": shifted(i)})

    for k in range(1, SIDE):
        pl.semaphore_signal(barrier, inc=1, device_id=peer_first(0, k)[1])
        pl.semaphore_signal(barrier, inc=1, device_id=peer_first(1, k)[1])
    pl.semaphore_wait(barrier, n_dp - 1 + 2 * (SIDE - 1))

    def remote(src, dst, send, recv, dev):
        return pltpu.make_async_remote_copy(
            src_ref=src, dst_ref=dst, send_sem=send, recv_sem=recv, device_id=dev
        )

    def start(copies):
        for c in copies:
            c.start()
        started.extend(copies)
        return copies

    def arrived(copies):
        for c in copies:
            c.wait_recv()

    def take(buf, sem):
        pltpu.make_async_copy(buf, buf, sem).wait()

    def weight_part(w, who):
        return w.at[who // quarters, :, pl.ds(mult(lax.rem(who, quarters) * hid, 128), hid)]

    def send_weights(n, w, own, lo, hi):
        @pl.loop(lo, hi)
        def _(i):
            who = shifted(i)
            remote(weight_part(w, who), own.at[j], w_send.at[n], w_recv.at[n], {"dp": who}).start()

    def send_tokens(n, msg, got):
        @pl.loop(1, blocks)
        def _(i):
            g = lax.rem(e + i, blocks)
            remote(msg.at[g], got.at[q, e], t_send.at[n], t_recv.at[n], {"dp": g * quarters + q}).start()

        pltpu.make_async_copy(msg.at[e], got.at[q, e], t_recv.at[n]).start()

    def relay_far(n, got):
        dev = {"dp": e * quarters + far_q}
        return start([remote(got.at[q], got.at[q], relay_send.at[n, 0], relay_recv.at[n, 0], dev)])

    def relay_near(n, got):
        dev = {"dp": e * quarters + near_q}
        return start(
            [
                remote(got.at[r], got.at[r], relay_send.at[n, 1 + i], relay_recv.at[n, 1 + i], dev)
                for i, r in enumerate((q, far_q))
            ]
        )

    def gather_rows(got, main, tail):
        @pl.loop(0, quarters)
        def _(r):
            for g in range(blocks):
                main[pl.ds(mult((r * blocks + g) * HEAD, HEAD), HEAD), :] = got[r, g, :HEAD, :]

        @pl.loop(0, blocks)
        def _(g):
            total = got[0, g, HEAD:, :].astype(F32)
            for r in range(1, quarters):
                total = total + got[r, g, HEAD:, :].astype(F32)
            tail32[pl.ds(mult(g * TAIL, TAIL), TAIL), :] = total

        tail[...] = tail32[...].astype(BF)

    def partial(t, main, tail, own):
        @pl.loop(0, hid // 256)
        def _(c):
            cols = pl.ds(mult(c * 256, 256), 256)
            w = own[:, :, cols].reshape(own_f, 256)
            pm[t, :, cols] = dot(main[...], w, 1, 0).astype(BF)
            pt[t, :, cols] = dot(tail[...], w, 1, 0).astype(BF)

    RIGHT, LEFT, FACING = 1, 3, 2
    hb, htb = big // 2, ht // 2

    def chunk_main(t, h, c, part):
        return pl.ds(mult(h * half_rows + c * big + part * hb, hb), hb)

    def chunk_tail(h, c, part):
        return pl.ds(h * ht + part * htb, htb), pl.ds(mult(c * wide, wide), wide)

    def rs_piece(t, h, to, c, part, dst_m, dst_t, n):
        dev = peer_first(h, to)[1]
        rows, cols = chunk_tail(h, c, part)
        return [
            remote(pm.at[t, chunk_main(t, h, c, part), :], dst_m, rs_send.at[t, h, n, 0], rs_recv.at[t, h, n, 0], dev),
            remote(pt.at[t, rows, cols], dst_t, rs_send.at[t, h, n, 1], rs_recv.at[t, h, n, 1], dev),
        ]

    def rs_pieces(t):
        passing, direct, joined = [], [], []
        for h in range(2):
            for side, to in enumerate((RIGHT, LEFT)):
                facing = peer_first(h, FACING)[0]
                c = peer_first(h, to)[0]
                passing.append(rs_piece(t, h, to, facing, side, ram.at[t, h, side], rat.at[t, h, side], side))
                direct.append(
                    rs_piece(t, h, to, c, 1 - side, rbm.at[t, h, side, 1 - side], rbt.at[t, h, side, 1 - side], 2 + side)
                )
                joined.append(
                    rs_piece(t, h, to, c, side, rbm.at[t, h, side, side], rbt.at[t, h, side, side], 4 + side)
                )
        return passing, direct, joined

    def rs_begin(t):
        passing, direct, joined = rs_pieces(t)
        for piece in passing + direct:
            start(piece)
        return passing, direct, joined

    def rs_join(t, pieces):
        passing, direct, joined = pieces
        n = 0
        for h in range(2):
            for side, to in enumerate((RIGHT, LEFT)):
                arrived(passing[n])
                c = peer_first(h, to)[0]
                base = h * half_rows + c * big + side * hb

                @pl.loop(0, hb // 16)
                def _(i):
                    rows = pl.ds(mult(base + i * 16, 16), 16)
                    got = ram[t, h, side, pl.ds(mult(i * 16, 16), 16), :]
                    pm[t, rows, :] = (pm[t, rows, :].astype(F32) + got.astype(F32)).astype(BF)

                rows, cols = chunk_tail(h, c, side)
                pt[t, rows, cols] = (pt[t, rows, cols].astype(F32) + rat[t, h, side].astype(F32)).astype(BF)
                start(joined[n])
                n += 1
        for piece in direct + joined:
            arrived(piece)

    def sum_first(t):
        for h in range(2):
            for part in range(2):
                base = h * half_rows + first(h) * big + part * hb

                @pl.loop(0, hb // 16)
                def _(i):
                    rows = pl.ds(mult(i * 16, 16), 16)
                    total = pm[t, pl.ds(mult(base + i * 16, 16), 16), :].astype(F32)
                    for side in range(2):
                        total = total + rbm[t, h, side, part, rows, :].astype(F32)
                    sm[t, h, pl.ds(mult(part * hb + i * 16, 16), 16), :] = total.astype(BF)

                rows, cols = chunk_tail(h, first(h), part)
                total = pt[t, rows, cols].astype(F32)
                for side in range(2):
                    total = total + rbt[t, h, side, part].astype(F32)
                st[t, h, part * htb : (part + 1) * htb, :] = total.astype(BF)

    def rs_small(t):
        out = []
        for h in range(2):
            for k in range(1, SIDE):
                c, dev = peer_second(h, k)
                sems = lambda n: (rs2_send.at[t, h, k - 1, n], rs2_recv.at[t, h, k - 1, n])
                out += [
                    remote(sm.at[t, h, pl.ds(mult(c * small, small), small), :], r2m.at[t, h, k - 1], *sems(0), dev),
                    remote(st.at[t, h, :, pl.ds(mult(c * narrow, narrow), narrow)], r2t.at[t, h, k - 1], *sems(1), dev),
                ]
        return start(out)

    def owned_rows(h):
        return pl.ds(mult(h * half_rows + first(h) * big + second(h) * small, small), small)

    def owned_cols(h):
        return pl.ds(mult(first(h) * wide + second(h) * narrow, narrow), narrow)

    def finish(t, fn):
        for h in range(2):

            @pl.loop(0, small // 16)
            def _(i):
                rows = pl.ds(mult(i * 16, 16), 16)
                total = sm[t, h, pl.ds(mult(second(h) * small + i * 16, 16), 16), :].astype(F32)
                for k in range(SIDE - 1):
                    total = total + r2m[t, h, k, rows, :].astype(F32)
                start_row = h * half_rows + first(h) * big + second(h) * small
                fm[t, pl.ds(mult(start_row + i * 16, 16), 16), :] = fn(total, pre_m.at[h, rows, :]).astype(BF)

            total = st[t, h, :, pl.ds(mult(second(h) * narrow, narrow), narrow)].astype(F32)
            for k in range(SIDE - 1):
                total = total + r2t[t, h, k].astype(F32)
            ft[t, pl.ds(h * ht, ht), owned_cols(h)] = fn(total, pre_t.at[h]).astype(BF)

    def silu(total, keep):
        keep[...] = total
        return total / (1.0 + jnp.exp(-total))

    def silu_back(total, keep):
        pre = keep[...]
        s = 1.0 / (1.0 + jnp.exp(-pre))
        return total * s * (1.0 + pre * (1.0 - s))

    def ag_small(t):
        out = []
        for h in range(2):
            for k in range(1, SIDE):
                dev = peer_second(h, k)[1]
                for n, ref in enumerate(
                    (fm.at[t, owned_rows(h), :], ft.at[t, pl.ds(h * ht, ht), owned_cols(h)])
                ):
                    out.append(remote(ref, ref, ag_send.at[t, h, k - 1, n], ag_recv.at[t, h, k - 1, n], dev))
        return start(out)

    def ag_piece(t, h, to, c, part, n):
        dev = peer_first(h, to)[1]
        rows, cols = chunk_tail(h, c, part)
        return [
            remote(ref, ref, ag2_send.at[t, h, n, i], ag2_recv.at[t, h, n, i], dev)
            for i, ref in enumerate((fm.at[t, chunk_main(t, h, c, part), :], ft.at[t, rows, cols]))
        ]

    def ag_big(t):
        early, late, passed = [], [], []
        for h in range(2):
            for side, to in enumerate((RIGHT, LEFT)):
                early.append(start(ag_piece(t, h, to, first(h), side, side)))
        for h in range(2):
            for side, to in enumerate((RIGHT, LEFT)):
                late.append(start(ag_piece(t, h, to, first(h), 1 - side, 2 + side)))
        n = 0
        for h in range(2):
            for side, to in enumerate((RIGHT, LEFT)):
                arrived(early[n])
                back_c = peer_first(h, LEFT if to == RIGHT else RIGHT)[0]
                passed.append(start(ag_piece(t, h, to, back_c, side, 4 + side)))
                n += 1
        return late + passed

    def settle(pieces):
        for piece in pieces:
            arrived(piece)

    def back(t, own):
        flat = own[...].reshape(own_f, hid)
        rows = blocks * HEAD

        @pl.loop(0, quarters)
        def _(r):
            part = dot(fm[t, pl.ds(mult(r * rows, rows), rows), :], flat, 1, 1).astype(BF)
            for g in range(blocks):
                back_msg[t, r, g, :HEAD, :] = part[g * HEAD : (g + 1) * HEAD, :]

        tail32[...] = dot(ft[t, :, :hid], flat, 1, 1)

        @pl.loop(0, blocks)
        def _(g):
            for r in range(quarters):
                back_msg[t, r, g, HEAD:, :] = tail32[pl.ds(mult(g * TAIL, TAIL), TAIL), :].astype(BF)

    def fold_near(t):
        dev = {"dp": e * quarters + near_q}
        return start(
            [
                remote(back_msg.at[t, r], sum_in.at[t, i], fold_send.at[t, i], fold_recv.at[t, i], dev)
                for i, r in enumerate((near_q, near_far_q))
            ]
        )

    def fold_far(t):
        for i, r in ((1, far_q), (0, q)):
            for g in range(blocks):
                total = back_msg[t, r, g].astype(F32) + sum_in[t, i, g].astype(F32)
                back_msg[t, r, g] = total.astype(BF)
            if i == 1:
                dev = {"dp": e * quarters + far_q}
                out = start(
                    [remote(back_msg.at[t, r], sum_far.at[t], fold_send.at[t, 2], fold_recv.at[t, 2], dev)]
                )
        return out

    def give_back(t, got):
        for g in range(blocks):
            total = back_msg[t, q, g].astype(F32) + sum_far[t, g].astype(F32)
            back_msg[t, q, g] = total.astype(BF)

        @pl.loop(1, blocks)
        def _(i):
            g = lax.rem(e + i, blocks)
            remote(back_msg.at[t, q, g], got.at[e], o_send.at[t], o_recv.at[t], {"dp": g * quarters + q}).start()

        pltpu.make_async_copy(back_msg.at[t, q, e], got.at[e], o_recv.at[t]).start()

    def gradient(main, tail, t, out):
        left_m, left_t = main[...], tail[...]

        @pl.loop(0, hid // 256)
        def _(c):
            cols = pl.ds(mult(c * 256, 256), 256)
            g = dot(left_m, fm[t, :, cols], 0, 0) + dot(left_t, ft[t, :, cols], 0, 0)
            out[:, cols] = g.astype(BF)

    send_tokens(0, x_msg, x_got)
    send_tokens(1, d_msg, d_got)
    send_weights(0, up, up_own, 0, 8)
    pltpu.make_async_copy(weight_part(up, j), up_own.at[j], w_recv.at[0]).start()
    pltpu.make_async_copy(weight_part(down, j), down_own.at[j], w_recv.at[1]).start()
    take(x_got.at[q], t_recv.at[0])
    xf = relay_far(0, x_got)
    take(d_got.at[q], t_recv.at[1])
    df = relay_far(1, d_got)
    send_weights(0, up, up_own, 8, n_dp - 1)
    arrived(xf)
    xn = relay_near(0, x_got)
    arrived(df)
    dn = relay_near(1, d_got)
    send_weights(1, down, down_own, 0, n_dp - 1)
    pt[:, :, hid:] = jnp.zeros((2, t_rows, pt.shape[2] - hid), BF)
    arrived(xn)
    gather_rows(x_got, xm, xt)
    arrived(dn)
    gather_rows(d_got, dm, dt)

    take(up_own, w_recv.at[0])
    partial(0, xm, xt, up_own)
    rs_join(0, rs_begin(0))
    sum_first(0)
    arrived(rs_small(0))
    finish(0, silu)
    arrived(ag_small(0))
    ag0 = ag_big(0)

    take(down_own, w_recv.at[1])
    partial(1, dm, dt, down_own)
    rs1 = rs_begin(1)
    settle(ag0)
    rs_join(1, rs1)
    sum_first(1)
    small1 = rs_small(1)
    back(0, down_own)
    near0 = fold_near(0)
    arrived(small1)
    finish(1, silu_back)
    gather1 = ag_small(1)
    arrived(near0)
    far0 = fold_far(0)
    arrived(gather1)
    ag1 = ag_big(1)
    arrived(far0)
    give_back(0, y_out)
    gradient(dm, dt, 0, gd_out)
    settle(ag1)
    back(1, up_own)
    near1 = fold_near(1)
    arrived(near1)
    far1 = fold_far(1)
    arrived(far1)
    give_back(1, dx_out)
    gradient(xm, xt, 1, gu_out)
    take(y_out, o_recv.at[0])
    take(dx_out, o_recv.at[1])
    for c in started:
        c.wait_send()
    for n, own in enumerate((up_own, down_own)):
        take(own.at[pl.ds(0, n_dp - 1)], w_send.at[n])
    for n, got in enumerate((x_got, d_got)):
        take(got.at[0, pl.ds(0, blocks - 1)], t_send.at[n])
    for n, got in enumerate((y_out, dx_out)):
        take(got.at[pl.ds(0, blocks - 1)], o_send.at[n])


def layer(x_msg, d_msg, up, down):
    n_dp = lax.axis_size("dp")
    own_f = x_msg.shape[2]
    rows = up.shape[1]
    quarters = n_dp // E
    blocks = n_dp // quarters
    hid = up.shape[2] // quarters
    main = n_dp * HEAD
    tails = blocks * TAIL
    wide = -(-hid // (SIDE * SIDE * 128)) * SIDE * SIDE * 128
    big = main // 2 // SIDE
    small = big // SIDE
    ht = tails // 2
    vm = pltpu.VMEM
    dma = pltpu.SemaphoreType.DMA
    return pl.pallas_call(
        layer_kernel,
        name="layer",
        out_shape=(
            jax.ShapeDtypeStruct((E, MSG, own_f), BF),
            jax.ShapeDtypeStruct((E, MSG, own_f), BF),
            jax.ShapeDtypeStruct((own_f, hid), BF),
            jax.ShapeDtypeStruct((own_f, hid), BF),
        ),
        in_specs=[pl.BlockSpec(memory_space=pltpu.VMEM)] * 2 + [pl.BlockSpec(memory_space=pl.ANY)] * 2,
        out_specs=[pl.BlockSpec(memory_space=pltpu.VMEM)] * 4,
        scratch_shapes=[
            vm((n_dp, rows, hid), BF), vm((n_dp, rows, hid), BF),
            vm((quarters, blocks, MSG, own_f), BF), vm((quarters, blocks, MSG, own_f), BF),
            vm((2, quarters, blocks, MSG, own_f), BF), vm((2, 2, blocks, MSG, own_f), BF),
            vm((2, blocks, MSG, own_f), BF),
            vm((main, own_f), BF), vm((tails, own_f), BF),
            vm((main, own_f), BF), vm((tails, own_f), BF),
            vm((tails, own_f), F32),
            vm((2, main, hid), BF), vm((2, tails, wide), BF),
            vm((2, 2, 2, big // 2, hid), BF), vm((2, 2, 2, ht // 2, wide // SIDE), BF),
            vm((2, 2, 2, 2, big // 2, hid), BF), vm((2, 2, 2, 2, ht // 2, wide // SIDE), BF),
            vm((2, 2, big, hid), BF), vm((2, 2, ht, wide // SIDE), BF),
            vm((2, 2, SIDE - 1, small, hid), BF), vm((2, 2, SIDE - 1, ht, wide // SIDE // SIDE), BF),
            vm((2, small, hid), F32), vm((2, ht, wide // SIDE // SIDE), F32),
            vm((2, main, hid), BF), vm((2, tails, wide), BF),
            dma((2,)), dma((2,)), dma((2,)), dma((2,)), dma((2, 3)), dma((2, 3)), dma((2, 3)), dma((2, 3)),
            dma((2,)), dma((2,)),
            dma((2, 2, 6, 2)), dma((2, 2, 6, 2)), dma((2, 2, SIDE - 1, 2)), dma((2, 2, SIDE - 1, 2)),
            dma((2, 2, SIDE - 1, 2)), dma((2, 2, SIDE - 1, 2)), dma((2, 2, 6, 2)), dma((2, 2, 6, 2)),
        ],
        compiler_params=pltpu.CompilerParams(
            collective_id=0, has_side_effects=True, vmem_limit_bytes=58 * 2**20
        ),
    )(x_msg, d_msg, up, down)


def body(tokens, routes, route_weights, up_stacked, down_stacked, cotangent):
    experts = jnp.arange(E, dtype=jnp.int32)
    named = routes[:, :, None] == experts[None, None, :]
    chosen = jnp.sum(named.astype(F32), axis=1)
    rows = jnp.arange(routes.shape[0], dtype=jnp.int32)
    earlier = (rows[None, :] < rows[:, None]).astype(BF)
    before = jnp.dot(earlier, chosen.astype(BF), preferred_element_type=F32).astype(jnp.int32)
    slot_pos = jnp.sum(jnp.where(named, before[:, None, :], 0), axis=2)
    shift = 2 * lax.rem(lax.axis_index("dp"), 4)
    target = routes * MSG + slot_pos + jnp.where(slot_pos >= HEAD, shift, 0)
    slot_hits = jnp.arange(E * MSG, dtype=jnp.int32)[:, None, None] == target[None, :, :]
    pick_table = jnp.sum(slot_hits.astype(F32), axis=2)
    weighted = jnp.sum(jnp.where(slot_hits, route_weights[None, :, :], 0.0), axis=2)
    features = tokens.shape[1]
    x_msg = jnp.dot(pick_table.astype(BF), tokens, preferred_element_type=F32).astype(BF)
    d_msg = jnp.dot(weighted, cotangent.astype(F32), precision=lax.Precision.HIGHEST).astype(BF)
    y_slots, dx_slots, g_up, g_down = layer(
        x_msg.reshape(E, MSG, features), d_msg.reshape(E, MSG, features), up_stacked, down_stacked
    )
    y_slots = y_slots.reshape(E * MSG, features).astype(F32)
    dx_slots = dx_slots.reshape(E * MSG, features).astype(F32)
    mixed = jnp.dot(weighted.T, y_slots, precision=lax.Precision.HIGHEST).astype(BF)
    grad_tokens = jnp.dot(pick_table.T, dx_slots, precision=lax.Precision.HIGHEST).astype(BF)
    return (mixed, grad_tokens, g_up[None], g_down[None])


def solution(mesh):
    placed = (
        P("dp", "member"),
        P("dp", None),
        P("dp", None),
        P(None, ("member", "dp"), None),
        P(None, ("member", "dp"), None),
        P("dp", "member"),
    )
    return jax.shard_map(
        body,
        mesh=mesh,
        in_specs=placed,
        out_specs=(
            P("dp", "member"),
            P("dp", "member"),
            P("dp", "member", None),
            P("dp", "member", None),
        ),
        check_vma=False,
    )
```

```python
import jax
import jax.numpy as jnp
from jax import lax
from jax.experimental import pallas as pl
from jax.experimental.pallas import tpu as pltpu
from jax.sharding import PartitionSpec as P

FF_W = 7168
E = 8
CAP = 34
SIDE = 4
PARTS = 2
HEAD = 32
TAIL = 8
MSG = HEAD + TAIL
BF = jnp.bfloat16
F32 = jnp.float32


def dot(a, b, ca, cb):
    return lax.dot_general(a, b, (((ca,), (cb,)), ((), ())), preferred_element_type=F32)


def mult(i, n):
    return pl.multiple_of(i, n)


def layer_kernel(
    x_msg, d_msg, up, down,
    y_out, dx_out, gu_out, gd_out,
    up_own, down_own, x_got, d_got, back_msg, sum_in, sum_far,
    xm, xt, dm, dt, tail32, early,
    pm, pt, ram, rat, rbm, rbt, sm, st, r2m, r2t, pre_m, pre_t, fm, ft,
    w_send, w_recv, t_send, t_recv, relay_send, relay_recv, fold_send, fold_recv, o_send, o_recv,
    rs_send, rs_recv, rs2_send, rs2_recv, ag_send, ag_recv, ag2_send, ag2_recv,
):
    n_dp = lax.axis_size("dp")
    quarters = n_dp // E
    blocks = n_dp // quarters
    hw = up_own.shape[3]
    hid = PARTS * hw
    last = PARTS - 1
    own_f = xm.shape[1]
    j = lax.axis_index("dp")
    m = lax.axis_index("member")
    e, q = j // quarters, lax.rem(j, quarters)
    far_q = lax.rem(q + 2, 4)
    near_q = q + 1 - 2 * lax.rem(q, 2)
    near_far_q = lax.rem(near_q + 2, 4)
    cy, cx = m // SIDE, lax.rem(m, SIDE)
    half_rows = n_dp * HEAD // 2
    big = half_rows // SIDE
    small = big // SIDE
    t_rows = blocks * TAIL
    ht = t_rows // 2
    wide = pt.shape[2] // SIDE
    narrow = wide // SIDE
    started = []

    def first(h):
        return cx if h == 0 else cy

    def second(h):
        return cy if h == 0 else cx

    def peer_first(h, k):
        c = lax.rem(first(h) + k, SIDE)
        return c, {"member": cy * SIDE + c if h == 0 else c * SIDE + cx}

    def peer_second(h, k):
        c = lax.rem(second(h) + k, SIDE)
        return c, {"member": c * SIDE + cx if h == 0 else cy * SIDE + c}

    def shifted(i):
        step = i // 2 + 1
        return lax.rem(j + n_dp + step * (1 - 2 * lax.rem(i, 2)), n_dp)

    barrier = pltpu.get_barrier_semaphore()

    @pl.loop(0, n_dp - 1)
    def _(i):
        pl.semaphore_signal(barrier, inc=1, device_id={"dp": shifted(i)})

    for k in range(1, SIDE):
        pl.semaphore_signal(barrier, inc=1, device_id=peer_first(0, k)[1])
        pl.semaphore_signal(barrier, inc=1, device_id=peer_first(1, k)[1])
    pl.semaphore_wait(barrier, n_dp - 1 + 2 * (SIDE - 1))

    def remote(src, dst, send, recv, dev):
        return pltpu.make_async_remote_copy(
            src_ref=src, dst_ref=dst, send_sem=send, recv_sem=recv, device_id=dev
        )

    def start(copies):
        for c in copies:
            c.start()
        started.extend(copies)
        return copies

    def arrived(copies):
        for c in copies:
            c.wait_recv()

    def take(buf, sem):
        pltpu.make_async_copy(buf, buf, sem).wait()

    def weight_part(w, u, who):
        column = lax.rem(who, quarters) * hid + u * hw
        return w.at[who // quarters, :, pl.ds(mult(column, 128), hw)]

    def send_weights(t, u, w, own, lo, hi):
        n = t * PARTS + u

        @pl.loop(lo, hi)
        def _(i):
            who = shifted(i)
            remote(weight_part(w, u, who), own.at[u, j], w_send.at[n], w_recv.at[n], {"dp": who}).start()

    def keep_weights(t, w, own):
        for u in range(PARTS):
            pltpu.make_async_copy(weight_part(w, u, j), own.at[u, j], w_recv.at[t * PARTS + u]).start()

    def send_tokens(n, msg, got):
        @pl.loop(1, blocks)
        def _(i):
            g = lax.rem(e + i, blocks)
            remote(msg.at[g], got.at[q, e], t_send.at[n], t_recv.at[n], {"dp": g * quarters + q}).start()

        pltpu.make_async_copy(msg.at[e], got.at[q, e], t_recv.at[n]).start()

    def relay_far(n, got):
        dev = {"dp": e * quarters + far_q}
        return start([remote(got.at[q], got.at[q], relay_send.at[n, 0], relay_recv.at[n, 0], dev)])

    def relay_near(n, got):
        dev = {"dp": e * quarters + near_q}
        return start(
            [
                remote(got.at[r], got.at[r], relay_send.at[n, 1 + i], relay_recv.at[n, 1 + i], dev)
                for i, r in enumerate((q, far_q))
            ]
        )

    def gather_rows(got, main, tail):
        @pl.loop(0, quarters)
        def _(r):
            for g in range(blocks):
                main[pl.ds(mult((r * blocks + g) * HEAD, HEAD), HEAD), :] = got[r, g, :HEAD, :]

        @pl.loop(0, blocks)
        def _(g):
            total = got[0, g, HEAD:, :].astype(F32)
            for r in range(1, quarters):
                total = total + got[r, g, HEAD:, :].astype(F32)
            tail32[pl.ds(mult(g * TAIL, TAIL), TAIL), :] = total

        tail[...] = tail32[...].astype(BF)

    def flat(own, u):
        return own[u].reshape(own_f, hw)

    def partial(t, u, main, tail, own):
        rows = n_dp * HEAD // 4

        @pl.loop(0, 4)
        def _(i):
            block = pl.ds(mult(i * rows, rows), rows)
            pm[t, u, block, :] = dot(main[block, :], flat(own, u), 1, 0).astype(BF)

        if u == last:
            for v in range(PARTS):
                pt[t, :, v * hw : (v + 1) * hw] = dot(tail[...], flat(own, v), 1, 0).astype(BF)

    RIGHT, LEFT, FACING = 1, 3, 2
    hb, htb = big // 2, ht // 2

    def chunk_main(h, c, part):
        return pl.ds(mult(h * half_rows + c * big + part * hb, hb), hb)

    def chunk_tail(h, c, part):
        return pl.ds(h * ht + part * htb, htb), pl.ds(mult(c * wide, wide), wide)

    def rs_piece(t, u, h, to, c, part, dst_m, dst_t, n):
        dev = peer_first(h, to)[1]
        p = t * PARTS + u
        src = pm.at[t, u, chunk_main(h, c, part), :]
        out = [remote(src, dst_m, rs_send.at[p, h, n, 0], rs_recv.at[p, h, n, 0], dev)]
        if u == last:
            rows, cols = chunk_tail(h, c, part)
            out.append(remote(pt.at[t, rows, cols], dst_t, rs_send.at[p, h, n, 1], rs_recv.at[p, h, n, 1], dev))
        return out

    def rs_begin(t, u):
        passing, direct, joined = [], [], []
        for h in range(2):
            for side, to in enumerate((RIGHT, LEFT)):
                facing = peer_first(h, FACING)[0]
                c = peer_first(h, to)[0]
                a, b = (ram.at[t, u, h, side], rat.at[t, h, side]), (rbm.at[t, u, h, side], rbt.at[t, h, side])
                passing.append(rs_piece(t, u, h, to, facing, side, *a, side))
                direct.append(rs_piece(t, u, h, to, c, 1 - side, b[0].at[1 - side], b[1].at[1 - side], 2 + side))
                joined.append(rs_piece(t, u, h, to, c, side, b[0].at[side], b[1].at[side], 4 + side))
        for piece in passing + direct:
            start(piece)
        return passing, direct, joined

    def rs_join(t, u, pieces):
        passing, direct, joined = pieces
        n = 0
        for h in range(2):
            for side, to in enumerate((RIGHT, LEFT)):
                arrived(passing[n])
                c = peer_first(h, to)[0]
                base = h * half_rows + c * big + side * hb

                @pl.loop(0, hb // 16)
                def _(i):
                    rows = pl.ds(mult(base + i * 16, 16), 16)
                    got = ram[t, u, h, side, pl.ds(mult(i * 16, 16), 16), :]
                    pm[t, u, rows, :] = (pm[t, u, rows, :].astype(F32) + got.astype(F32)).astype(BF)

                if u == last:
                    rows, cols = chunk_tail(h, c, side)
                    pt[t, rows, cols] = (pt[t, rows, cols].astype(F32) + rat[t, h, side].astype(F32)).astype(BF)
                start(joined[n])
                n += 1
        for piece in direct + joined:
            arrived(piece)

    def sum_first(t, u):
        for h in range(2):
            for part in range(2):
                base = h * half_rows + first(h) * big + part * hb

                @pl.loop(0, hb // 16)
                def _(i):
                    rows = pl.ds(mult(i * 16, 16), 16)
                    total = pm[t, u, pl.ds(mult(base + i * 16, 16), 16), :].astype(F32)
                    for side in range(2):
                        total = total + rbm[t, u, h, side, part, rows, :].astype(F32)
                    sm[t, u, h, pl.ds(mult(part * hb + i * 16, 16), 16), :] = total.astype(BF)

                if u == last:
                    rows, cols = chunk_tail(h, first(h), part)
                    total = pt[t, rows, cols].astype(F32)
                    for side in range(2):
                        total = total + rbt[t, h, side, part].astype(F32)
                    st[t, h, part * htb : (part + 1) * htb, :] = total.astype(BF)

    def rs_small(t, u):
        out = []
        p = t * PARTS + u
        for h in range(2):
            for k in range(1, SIDE):
                c, dev = peer_second(h, k)
                pairs = [(sm.at[t, u, h, pl.ds(mult(c * small, small), small), :], r2m.at[t, u, h, k - 1])]
                if u == last:
                    pairs.append((st.at[t, h, :, pl.ds(mult(c * narrow, narrow), narrow)], r2t.at[t, h, k - 1]))
                for n, (src, dst) in enumerate(pairs):
                    out.append(remote(src, dst, rs2_send.at[p, h, k - 1, n], rs2_recv.at[p, h, k - 1, n], dev))
        return start(out)

    def owned_rows(h):
        return pl.ds(mult(h * half_rows + first(h) * big + second(h) * small, small), small)

    def owned_cols(h):
        return pl.ds(mult(first(h) * wide + second(h) * narrow, narrow), narrow)

    def finish(t, u, fn):
        for h in range(2):

            @pl.loop(0, small // 16)
            def _(i):
                rows = pl.ds(mult(i * 16, 16), 16)
                total = sm[t, u, h, pl.ds(mult(second(h) * small + i * 16, 16), 16), :].astype(F32)
                for k in range(SIDE - 1):
                    total = total + r2m[t, u, h, k, rows, :].astype(F32)
                start_row = h * half_rows + first(h) * big + second(h) * small
                fm[t, u, pl.ds(mult(start_row + i * 16, 16), 16), :] = fn(total, pre_m.at[u, h, rows, :]).astype(BF)

            if u == last:
                total = st[t, h, :, pl.ds(mult(second(h) * narrow, narrow), narrow)].astype(F32)
                for k in range(SIDE - 1):
                    total = total + r2t[t, h, k].astype(F32)
                ft[t, pl.ds(h * ht, ht), owned_cols(h)] = fn(total, pre_t.at[h]).astype(BF)

    def silu(total, keep):
        keep[...] = total
        return total / (1.0 + jnp.exp(-total))

    def silu_back(total, keep):
        pre = keep[...]
        s = 1.0 / (1.0 + jnp.exp(-pre))
        return total * s * (1.0 + pre * (1.0 - s))

    def ag_small(t, u):
        out = []
        p = t * PARTS + u
        for h in range(2):
            for k in range(1, SIDE):
                dev = peer_second(h, k)[1]
                refs = [fm.at[t, u, owned_rows(h), :]]
                if u == last:
                    refs.append(ft.at[t, pl.ds(h * ht, ht), owned_cols(h)])
                for n, ref in enumerate(refs):
                    out.append(remote(ref, ref, ag_send.at[p, h, k - 1, n], ag_recv.at[p, h, k - 1, n], dev))
        return start(out)

    def ag_piece(t, u, h, to, c, part, n):
        dev = peer_first(h, to)[1]
        p = t * PARTS + u
        refs = [fm.at[t, u, chunk_main(h, c, part), :]]
        if u == last:
            rows, cols = chunk_tail(h, c, part)
            refs.append(ft.at[t, rows, cols])
        return [
            remote(ref, ref, ag2_send.at[p, h, n, i], ag2_recv.at[p, h, n, i], dev) for i, ref in enumerate(refs)
        ]

    def ag_big(t, u):
        soon, late = [], []
        for h in range(2):
            for side, to in enumerate((RIGHT, LEFT)):
                soon.append(start(ag_piece(t, u, h, to, first(h), side, side)))
        for h in range(2):
            for side, to in enumerate((RIGHT, LEFT)):
                late.append(start(ag_piece(t, u, h, to, first(h), 1 - side, 2 + side)))
        return soon, late

    def ag_pass(t, u, pieces):
        soon, late = pieces
        passed = []
        n = 0
        for h in range(2):
            for side, to in enumerate((RIGHT, LEFT)):
                arrived(soon[n])
                back_c = peer_first(h, LEFT if to == RIGHT else RIGHT)[0]
                passed.append(start(ag_piece(t, u, h, to, back_c, side, 4 + side)))
                n += 1
        return late + passed

    def settle(pieces):
        for piece in pieces:
            arrived(piece)

    share = blocks * HEAD

    def share_rows(r):
        return pl.ds(mult(r * share, share), share)

    def back_early(t, own):
        @pl.loop(0, quarters)
        def _(r):
            total = dot(fm[t, 0, share_rows(r), :], flat(own, 0), 1, 1)
            for u in range(1, last):
                total = total + dot(fm[t, u, share_rows(r), :], flat(own, u), 1, 1)
            early[share_rows(r), :] = total

    def back_tail(t, own):
        total = dot(ft[t, :, :hw], flat(own, 0), 1, 1)
        for u in range(1, PARTS):
            total = total + dot(ft[t, :, u * hw : (u + 1) * hw], flat(own, u), 1, 1)
        tail32[...] = total

    def back_share(t, own, r):
        total = early[share_rows(r), :] + dot(fm[t, last, share_rows(r), :], flat(own, last), 1, 1)
        part = total.astype(BF)
        for g in range(blocks):
            back_msg[t, r, g, :HEAD, :] = part[g * HEAD : (g + 1) * HEAD, :]
            back_msg[t, r, g, HEAD:, :] = tail32[g * TAIL : (g + 1) * TAIL, :].astype(BF)

    def fold_near(t, own):
        dev = {"dp": e * quarters + near_q}
        out = []
        for i, r in ((1, near_far_q), (0, near_q)):
            back_share(t, own, r)
            out += start([remote(back_msg.at[t, r], sum_in.at[t, i], fold_send.at[t, i], fold_recv.at[t, i], dev)])
        for r in (far_q, q):
            back_share(t, own, r)
        return out

    def fold_far(t, near):
        for n, (i, r) in enumerate(((1, far_q), (0, q))):
            arrived(near[n : n + 1])
            for g in range(blocks):
                total = back_msg[t, r, g].astype(F32) + sum_in[t, i, g].astype(F32)
                back_msg[t, r, g] = total.astype(BF)
            if i == 1:
                dev = {"dp": e * quarters + far_q}
                out = start(
                    [remote(back_msg.at[t, r], sum_far.at[t], fold_send.at[t, 2], fold_recv.at[t, 2], dev)]
                )
        return out

    def give_back(t, got):
        for g in range(blocks):
            total = back_msg[t, q, g].astype(F32) + sum_far[t, g].astype(F32)
            back_msg[t, q, g] = total.astype(BF)

        @pl.loop(1, blocks)
        def _(i):
            g = lax.rem(e + i, blocks)
            remote(back_msg.at[t, q, g], got.at[e], o_send.at[t], o_recv.at[t], {"dp": g * quarters + q}).start()

        pltpu.make_async_copy(back_msg.at[t, q, e], got.at[e], o_recv.at[t]).start()

    def gradient(main, tail, t, u, out):
        @pl.loop(0, hw // 128)
        def _(c):
            at = mult(c * 128, 128)
            g = dot(main[...], fm[t, u, :, pl.ds(at, 128)], 0, 0)
            g = g + dot(tail[...], ft[t, :, pl.ds(u * hw + at, 128)], 0, 0)
            out[:, pl.ds(u * hw + at, 128)] = g.astype(BF)

    send_tokens(0, x_msg, x_got)
    send_weights(0, 0, up, up_own, 0, 8)
    keep_weights(0, up, up_own)
    keep_weights(1, down, down_own)
    take(x_got.at[q], t_recv.at[0])
    xf = relay_far(0, x_got)
    send_weights(0, 0, up, up_own, 8, n_dp - 1)
    arrived(xf)
    xn = relay_near(0, x_got)
    send_weights(0, 1, up, up_own, 0, n_dp - 1)
    pt[:, :, hid:] = jnp.zeros((2, t_rows, pt.shape[2] - hid), BF)
    arrived(xn)
    gather_rows(x_got, xm, xt)

    take(up_own.at[0], w_recv.at[0])
    partial(0, 0, xm, xt, up_own)
    rs_0 = rs_begin(0, 0)
    send_tokens(1, d_msg, d_got)
    send_weights(1, 0, down, down_own, 0, n_dp - 1)
    rs_join(0, 0, rs_0)
    sum_first(0, 0)
    small_0 = rs_small(0, 0)

    take(up_own.at[1], w_recv.at[1])
    partial(0, 1, xm, xt, up_own)
    rs_1 = rs_begin(0, 1)
    take(d_got.at[q], t_recv.at[1])
    df = relay_far(1, d_got)
    arrived(small_0)
    finish(0, 0, silu)
    gather_0 = ag_small(0, 0)
    send_weights(1, 1, down, down_own, 0, n_dp - 1)
    rs_join(0, 1, rs_1)
    sum_first(0, 1)
    small_1 = rs_small(0, 1)
    arrived(gather_0)
    ag_0 = ag_big(0, 0)
    arrived(df)
    dn = relay_near(1, d_got)
    arrived(dn)
    gather_rows(d_got, dm, dt)

    take(down_own.at[0], w_recv.at[2])
    partial(1, 0, dm, dt, down_own)
    rs_2 = rs_begin(1, 0)
    arrived(small_1)
    finish(0, 1, silu)
    gather_1 = ag_small(0, 1)
    rest_0 = ag_pass(0, 0, ag_0)
    rs_join(1, 0, rs_2)
    sum_first(1, 0)
    small_2 = rs_small(1, 0)
    arrived(gather_1)
    ag_1 = ag_big(0, 1)

    take(down_own.at[1], w_recv.at[3])
    partial(1, 1, dm, dt, down_own)
    rs_3 = rs_begin(1, 1)
    arrived(small_2)
    finish(1, 0, silu_back)
    gather_2 = ag_small(1, 0)
    rest_1 = ag_pass(0, 1, ag_1)
    settle(rest_0)
    rs_join(1, 1, rs_3)
    sum_first(1, 1)
    small_3 = rs_small(1, 1)
    arrived(gather_2)
    ag_2 = ag_big(1, 0)
    back_early(0, down_own)
    settle(rest_1)
    back_tail(0, down_own)
    near_0 = fold_near(0, down_own)
    arrived(small_3)
    finish(1, 1, silu_back)
    gather_3 = ag_small(1, 1)
    rest_2 = ag_pass(1, 0, ag_2)
    far_0 = fold_far(0, near_0)
    arrived(gather_3)
    ag_3 = ag_big(1, 1)
    arrived(far_0)
    give_back(0, y_out)
    rest_3 = ag_pass(1, 1, ag_3)
    settle(rest_2)
    back_early(1, up_own)
    gradient(dm, dt, 0, 0, gd_out)
    gradient(dm, dt, 0, 1, gd_out)
    settle(rest_3)
    back_tail(1, up_own)
    near_1 = fold_near(1, up_own)
    far_1 = fold_far(1, near_1)
    arrived(far_1)
    give_back(1, dx_out)
    gradient(xm, xt, 1, 0, gu_out)
    gradient(xm, xt, 1, 1, gu_out)
    take(y_out, o_recv.at[0])
    take(dx_out, o_recv.at[1])
    for c in started:
        c.wait_send()
    for t, own in enumerate((up_own, down_own)):
        for u in range(PARTS):
            take(own.at[u, pl.ds(0, n_dp - 1)], w_send.at[t * PARTS + u])
    for n, got in enumerate((x_got, d_got)):
        take(got.at[0, pl.ds(0, blocks - 1)], t_send.at[n])
    for n, got in enumerate((y_out, dx_out)):
        take(got.at[pl.ds(0, blocks - 1)], o_send.at[n])


def layer(x_msg, d_msg, up, down):
    n_dp = lax.axis_size("dp")
    own_f = x_msg.shape[2]
    rows = up.shape[1]
    quarters = n_dp // E
    blocks = n_dp // quarters
    hid = up.shape[2] // quarters
    hw = hid // PARTS
    main = n_dp * HEAD
    tails = blocks * TAIL
    wide = -(-hid // (SIDE * SIDE * 128)) * SIDE * SIDE * 128
    big = main // 2 // SIDE
    small = big // SIDE
    ht = tails // 2
    vm = pltpu.VMEM
    dma = pltpu.SemaphoreType.DMA
    return pl.pallas_call(
        layer_kernel,
        name="layer",
        out_shape=(
            jax.ShapeDtypeStruct((E, MSG, own_f), BF),
            jax.ShapeDtypeStruct((E, MSG, own_f), BF),
            jax.ShapeDtypeStruct((own_f, hid), BF),
            jax.ShapeDtypeStruct((own_f, hid), BF),
        ),
        in_specs=[pl.BlockSpec(memory_space=pltpu.VMEM)] * 2 + [pl.BlockSpec(memory_space=pl.ANY)] * 2,
        out_specs=[pl.BlockSpec(memory_space=pltpu.VMEM)] * 4,
        scratch_shapes=[
            vm((PARTS, n_dp, rows, hw), BF), vm((PARTS, n_dp, rows, hw), BF),
            vm((quarters, blocks, MSG, own_f), BF), vm((quarters, blocks, MSG, own_f), BF),
            vm((2, quarters, blocks, MSG, own_f), BF), vm((2, 2, blocks, MSG, own_f), BF),
            vm((2, blocks, MSG, own_f), BF),
            vm((main, own_f), BF), vm((tails, own_f), BF),
            vm((main, own_f), BF), vm((tails, own_f), BF),
            vm((tails, own_f), F32), vm((main, own_f), F32),
            vm((2, PARTS, main, hw), BF), vm((2, tails, wide), BF),
            vm((2, PARTS, 2, 2, big // 2, hw), BF), vm((2, 2, 2, ht // 2, wide // SIDE), BF),
            vm((2, PARTS, 2, 2, 2, big // 2, hw), BF), vm((2, 2, 2, 2, ht // 2, wide // SIDE), BF),
            vm((2, PARTS, 2, big, hw), BF), vm((2, 2, ht, wide // SIDE), BF),
            vm((2, PARTS, 2, SIDE - 1, small, hw), BF), vm((2, 2, SIDE - 1, ht, wide // SIDE // SIDE), BF),
            vm((PARTS, 2, small, hw), F32), vm((2, ht, wide // SIDE // SIDE), F32),
            vm((2, PARTS, main, hw), BF), vm((2, tails, wide), BF),
            dma((2 * PARTS,)), dma((2 * PARTS,)), dma((2,)), dma((2,)),
            dma((2, 3)), dma((2, 3)), dma((2, 3)), dma((2, 3)), dma((2,)), dma((2,)),
            dma((2 * PARTS, 2, 6, 2)), dma((2 * PARTS, 2, 6, 2)),
            dma((2 * PARTS, 2, SIDE - 1, 2)), dma((2 * PARTS, 2, SIDE - 1, 2)),
            dma((2 * PARTS, 2, SIDE - 1, 2)), dma((2 * PARTS, 2, SIDE - 1, 2)),
            dma((2 * PARTS, 2, 6, 2)), dma((2 * PARTS, 2, 6, 2)),
        ],
        compiler_params=pltpu.CompilerParams(
            collective_id=0, has_side_effects=True, vmem_limit_bytes=58 * 2**20
        ),
    )(x_msg, d_msg, up, down)


def body(tokens, routes, route_weights, up_stacked, down_stacked, cotangent):
    experts = jnp.arange(E, dtype=jnp.int32)
    named = routes[:, :, None] == experts[None, None, :]
    chosen = jnp.sum(named.astype(F32), axis=1)
    rows = jnp.arange(routes.shape[0], dtype=jnp.int32)
    earlier = (rows[None, :] < rows[:, None]).astype(BF)
    before = jnp.dot(earlier, chosen.astype(BF), preferred_element_type=F32).astype(jnp.int32)
    slot_pos = jnp.sum(jnp.where(named, before[:, None, :], 0), axis=2)
    shift = 2 * lax.rem(lax.axis_index("dp"), 4)
    target = routes * MSG + slot_pos + jnp.where(slot_pos >= HEAD, shift, 0)
    slot_hits = jnp.arange(E * MSG, dtype=jnp.int32)[:, None, None] == target[None, :, :]
    pick_table = jnp.sum(slot_hits.astype(F32), axis=2)
    weighted = jnp.sum(jnp.where(slot_hits, route_weights[None, :, :], 0.0), axis=2)
    features = tokens.shape[1]
    x_msg = jnp.dot(pick_table.astype(BF), tokens, preferred_element_type=F32).astype(BF)
    d_msg = jnp.dot(weighted, cotangent.astype(F32), precision=lax.Precision.HIGHEST).astype(BF)
    y_slots, dx_slots, g_up, g_down = layer(
        x_msg.reshape(E, MSG, features), d_msg.reshape(E, MSG, features), up_stacked, down_stacked
    )
    y_slots = y_slots.reshape(E * MSG, features).astype(F32)
    dx_slots = dx_slots.reshape(E * MSG, features).astype(F32)
    mixed = jnp.dot(weighted.T, y_slots, precision=lax.Precision.HIGHEST).astype(BF)
    grad_tokens = jnp.dot(pick_table.T, dx_slots, precision=lax.Precision.HIGHEST).astype(BF)
    return (mixed, grad_tokens, g_up[None], g_down[None])


def solution(mesh):
    placed = (
        P("dp", "member"),
        P("dp", None),
        P("dp", None),
        P(None, ("member", "dp"), None),
        P(None, ("member", "dp"), None),
        P("dp", "member"),
    )
    return jax.shard_map(
        body,
        mesh=mesh,
        in_specs=placed,
        out_specs=(
            P("dp", "member"),
            P("dp", "member"),
            P("dp", "member", None),
            P("dp", "member", None),
        ),
        check_vma=False,
    )
```

```python
import jax
import jax.numpy as jnp
from jax import lax
from jax.experimental import pallas as pl
from jax.experimental.pallas import tpu as pltpu
from jax.sharding import PartitionSpec as P

FF_W = 7168
E = 8
CAP = 34
SIDE = 4
PARTS = 2
HEAD = 32
TAIL = 8
MSG = HEAD + TAIL
BF = jnp.bfloat16
F32 = jnp.float32


def dot(a, b, ca, cb):
    return lax.dot_general(a, b, (((ca,), (cb,)), ((), ())), preferred_element_type=F32)


def mult(i, n):
    return pl.multiple_of(i, n)


def layer_kernel(
    x_msg, d_msg, weighted, pick, up, down,
    mixed_out, gt_out, gu_out, gd_out,
    y_got, dx_got,
    up_own, down_own, x_got, d_got, back_msg, sum_in, sum_far,
    xm, xt, dm, dt, tail32, early,
    pm, pt, ram, rat, rbm, rbt, sm, st, r2m, r2t, pre_m, pre_t, fm, ft,
    w_send, w_recv, t_send, t_recv, relay_send, relay_recv, fold_send, fold_recv, o_send, o_recv,
    rs_send, rs_recv, rs2_send, rs2_recv, ag_send, ag_recv, ag2_send, ag2_recv,
):
    n_dp = lax.axis_size("dp")
    quarters = n_dp // E
    blocks = n_dp // quarters
    hw = up_own.shape[3]
    hid = PARTS * hw
    last = PARTS - 1
    own_f = xm.shape[1]
    j = lax.axis_index("dp")
    m = lax.axis_index("member")
    e, q = j // quarters, lax.rem(j, quarters)
    far_q = lax.rem(q + 2, 4)
    near_q = q + 1 - 2 * lax.rem(q, 2)
    near_far_q = lax.rem(near_q + 2, 4)
    cy, cx = m // SIDE, lax.rem(m, SIDE)
    half_rows = n_dp * HEAD // 2
    big = half_rows // SIDE
    small = big // SIDE
    t_rows = blocks * TAIL
    ht = t_rows // 2
    wide = pt.shape[2] // SIDE
    narrow = wide // SIDE
    started = []

    def first(h):
        return cx if h == 0 else cy

    def second(h):
        return cy if h == 0 else cx

    def peer_first(h, k):
        c = lax.rem(first(h) + k, SIDE)
        return c, {"member": cy * SIDE + c if h == 0 else c * SIDE + cx}

    def peer_second(h, k):
        c = lax.rem(second(h) + k, SIDE)
        return c, {"member": c * SIDE + cx if h == 0 else cy * SIDE + c}

    def shifted(i):
        step = i // 2 + 1
        return lax.rem(j + n_dp + step * (1 - 2 * lax.rem(i, 2)), n_dp)

    barrier = pltpu.get_barrier_semaphore()

    @pl.loop(0, n_dp - 1)
    def _(i):
        pl.semaphore_signal(barrier, inc=1, device_id={"dp": shifted(i)})

    for k in range(1, SIDE):
        pl.semaphore_signal(barrier, inc=1, device_id=peer_first(0, k)[1])
        pl.semaphore_signal(barrier, inc=1, device_id=peer_first(1, k)[1])
    pl.semaphore_wait(barrier, n_dp - 1 + 2 * (SIDE - 1))

    def remote(src, dst, send, recv, dev):
        return pltpu.make_async_remote_copy(
            src_ref=src, dst_ref=dst, send_sem=send, recv_sem=recv, device_id=dev
        )

    def start(copies):
        for c in copies:
            c.start()
        started.extend(copies)
        return copies

    def drain(count):
        for c in started[:count]:
            c.wait_send()
        del started[:count]

    def arrived(copies):
        for c in copies:
            c.wait_recv()

    def take(buf, sem):
        pltpu.make_async_copy(buf, buf, sem).wait()

    def weight_part(w, u, who):
        column = lax.rem(who, quarters) * hid + u * hw
        return w.at[who // quarters, :, pl.ds(mult(column, 128), hw)]

    def send_weights(t, u, w, own, lo, hi):
        n = t * PARTS + u

        @pl.loop(lo, hi)
        def _(i):
            who = shifted(i)
            remote(weight_part(w, u, who), own.at[u, j], w_send.at[n], w_recv.at[n], {"dp": who}).start()

    def keep_weights(t, w, own):
        for u in range(PARTS):
            pltpu.make_async_copy(weight_part(w, u, j), own.at[u, j], w_recv.at[t * PARTS + u]).start()

    def send_tokens(n, msg, got):
        @pl.loop(1, blocks)
        def _(i):
            g = lax.rem(e + i, blocks)
            remote(msg.at[g], got.at[q, e], t_send.at[n], t_recv.at[n], {"dp": g * quarters + q}).start()

        pltpu.make_async_copy(msg.at[e], got.at[q, e], t_recv.at[n]).start()

    def relay_far(n, got):
        dev = {"dp": e * quarters + far_q}
        return start([remote(got.at[q], got.at[q], relay_send.at[n, 0], relay_recv.at[n, 0], dev)])

    def relay_near(n, got):
        dev = {"dp": e * quarters + near_q}
        return start(
            [
                remote(got.at[r], got.at[r], relay_send.at[n, 1 + i], relay_recv.at[n, 1 + i], dev)
                for i, r in enumerate((q, far_q))
            ]
        )

    def gather_rows(got, main, tail):
        @pl.loop(0, quarters)
        def _(r):
            for g in range(blocks):
                main[pl.ds(mult((r * blocks + g) * HEAD, HEAD), HEAD), :] = got[r, g, :HEAD, :]

        @pl.loop(0, blocks)
        def _(g):
            total = got[0, g, HEAD:, :].astype(F32)
            for r in range(1, quarters):
                total = total + got[r, g, HEAD:, :].astype(F32)
            tail32[pl.ds(mult(g * TAIL, TAIL), TAIL), :] = total

        tail[...] = tail32[...].astype(BF)

    def flat(own, u):
        return own[u].reshape(own_f, hw)

    def partial(t, u, main, tail, own):
        rows = n_dp * HEAD // 4

        @pl.loop(0, 4)
        def _(i):
            block = pl.ds(mult(i * rows, rows), rows)
            pm[t, u, block, :] = dot(main[block, :], flat(own, u), 1, 0).astype(BF)

        if u == last:
            for v in range(PARTS):
                pt[t, :, v * hw : (v + 1) * hw] = dot(tail[...], flat(own, v), 1, 0).astype(BF)

    RIGHT, LEFT, FACING = 1, 3, 2
    hb, htb = big // 2, ht // 2

    def chunk_main(h, c, part):
        return pl.ds(mult(h * half_rows + c * big + part * hb, hb), hb)

    def chunk_tail(h, c, part):
        return pl.ds(h * ht + part * htb, htb), pl.ds(mult(c * wide, wide), wide)

    def rs_piece(t, u, h, to, c, part, dst_m, dst_t, n):
        dev = peer_first(h, to)[1]
        p = t * PARTS + u
        src = pm.at[t, u, chunk_main(h, c, part), :]
        out = [remote(src, dst_m, rs_send.at[p, h, n, 0], rs_recv.at[p, h, n, 0], dev)]
        if u == last:
            rows, cols = chunk_tail(h, c, part)
            out.append(remote(pt.at[t, rows, cols], dst_t, rs_send.at[p, h, n, 1], rs_recv.at[p, h, n, 1], dev))
        return out

    def rs_begin(t, u):
        passing, direct, joined = [], [], []
        for h in range(2):
            for side, to in enumerate((RIGHT, LEFT)):
                facing = peer_first(h, FACING)[0]
                c = peer_first(h, to)[0]
                a, b = (ram.at[t, u, h, side], rat.at[t, h, side]), (rbm.at[t, u, h, side], rbt.at[t, h, side])
                passing.append(rs_piece(t, u, h, to, facing, side, *a, side))
                direct.append(rs_piece(t, u, h, to, c, 1 - side, b[0].at[1 - side], b[1].at[1 - side], 2 + side))
                joined.append(rs_piece(t, u, h, to, c, side, b[0].at[side], b[1].at[side], 4 + side))
        for piece in passing + direct:
            start(piece)
        return passing, direct, joined

    def rs_join(t, u, pieces):
        passing, direct, joined = pieces
        n = 0
        for h in range(2):
            for side, to in enumerate((RIGHT, LEFT)):
                arrived(passing[n])
                c = peer_first(h, to)[0]
                base = h * half_rows + c * big + side * hb

                @pl.loop(0, hb // 16)
                def _(i):
                    rows = pl.ds(mult(base + i * 16, 16), 16)
                    got = ram[t, u, h, side, pl.ds(mult(i * 16, 16), 16), :]
                    pm[t, u, rows, :] = (pm[t, u, rows, :].astype(F32) + got.astype(F32)).astype(BF)

                if u == last:
                    rows, cols = chunk_tail(h, c, side)
                    pt[t, rows, cols] = (pt[t, rows, cols].astype(F32) + rat[t, h, side].astype(F32)).astype(BF)
                start(joined[n])
                n += 1
        for piece in direct + joined:
            arrived(piece)

    def sum_first(t, u):
        for h in range(2):
            for part in range(2):
                base = h * half_rows + first(h) * big + part * hb

                @pl.loop(0, hb // 16)
                def _(i):
                    rows = pl.ds(mult(i * 16, 16), 16)
                    total = pm[t, u, pl.ds(mult(base + i * 16, 16), 16), :].astype(F32)
                    for side in range(2):
                        total = total + rbm[t, u, h, side, part, rows, :].astype(F32)
                    sm[t, u, h, pl.ds(mult(part * hb + i * 16, 16), 16), :] = total.astype(BF)

                if u == last:
                    rows, cols = chunk_tail(h, first(h), part)
                    total = pt[t, rows, cols].astype(F32)
                    for side in range(2):
                        total = total + rbt[t, h, side, part].astype(F32)
                    st[t, h, part * htb : (part + 1) * htb, :] = total.astype(BF)

    def rs_small(t, u):
        out = []
        p = t * PARTS + u
        for h in range(2):
            for k in range(1, SIDE):
                c, dev = peer_second(h, k)
                pairs = [(sm.at[t, u, h, pl.ds(mult(c * small, small), small), :], r2m.at[t, u, h, k - 1])]
                if u == last:
                    pairs.append((st.at[t, h, :, pl.ds(mult(c * narrow, narrow), narrow)], r2t.at[t, h, k - 1]))
                for n, (src, dst) in enumerate(pairs):
                    out.append(remote(src, dst, rs2_send.at[p, h, k - 1, n], rs2_recv.at[p, h, k - 1, n], dev))
        return start(out)

    def owned_rows(h):
        return pl.ds(mult(h * half_rows + first(h) * big + second(h) * small, small), small)

    def owned_cols(h):
        return pl.ds(mult(first(h) * wide + second(h) * narrow, narrow), narrow)

    def finish(t, u, fn):
        for h in range(2):

            @pl.loop(0, small // 16)
            def _(i):
                rows = pl.ds(mult(i * 16, 16), 16)
                total = sm[t, u, h, pl.ds(mult(second(h) * small + i * 16, 16), 16), :].astype(F32)
                for k in range(SIDE - 1):
                    total = total + r2m[t, u, h, k, rows, :].astype(F32)
                start_row = h * half_rows + first(h) * big + second(h) * small
                fm[t, u, pl.ds(mult(start_row + i * 16, 16), 16), :] = fn(total, pre_m.at[u, h, rows, :]).astype(BF)

            if u == last:
                total = st[t, h, :, pl.ds(mult(second(h) * narrow, narrow), narrow)].astype(F32)
                for k in range(SIDE - 1):
                    total = total + r2t[t, h, k].astype(F32)
                ft[t, pl.ds(h * ht, ht), owned_cols(h)] = fn(total, pre_t.at[h]).astype(BF)

    def silu(total, keep):
        keep[...] = total
        return total / (1.0 + jnp.exp(-total))

    def silu_back(total, keep):
        pre = keep[...]
        s = 1.0 / (1.0 + jnp.exp(-pre))
        return total * s * (1.0 + pre * (1.0 - s))

    def ag_small(t, u):
        out = []
        p = t * PARTS + u
        for h in range(2):
            for k in range(1, SIDE):
                dev = peer_second(h, k)[1]
                refs = [fm.at[t, u, owned_rows(h), :]]
                if u == last:
                    refs.append(ft.at[t, pl.ds(h * ht, ht), owned_cols(h)])
                for n, ref in enumerate(refs):
                    out.append(remote(ref, ref, ag_send.at[p, h, k - 1, n], ag_recv.at[p, h, k - 1, n], dev))
        return start(out)

    def ag_piece(t, u, h, to, c, part, n):
        dev = peer_first(h, to)[1]
        p = t * PARTS + u
        refs = [fm.at[t, u, chunk_main(h, c, part), :]]
        if u == last:
            rows, cols = chunk_tail(h, c, part)
            refs.append(ft.at[t, rows, cols])
        return [
            remote(ref, ref, ag2_send.at[p, h, n, i], ag2_recv.at[p, h, n, i], dev) for i, ref in enumerate(refs)
        ]

    def ag_big(t, u):
        soon, late = [], []
        for h in range(2):
            for side, to in enumerate((RIGHT, LEFT)):
                soon.append(start(ag_piece(t, u, h, to, first(h), side, side)))
        for h in range(2):
            for side, to in enumerate((RIGHT, LEFT)):
                late.append(start(ag_piece(t, u, h, to, first(h), 1 - side, 2 + side)))
        return soon, late

    def ag_pass(t, u, pieces):
        soon, late = pieces
        passed = []
        n = 0
        for h in range(2):
            for side, to in enumerate((RIGHT, LEFT)):
                arrived(soon[n])
                back_c = peer_first(h, LEFT if to == RIGHT else RIGHT)[0]
                passed.append(start(ag_piece(t, u, h, to, back_c, side, 4 + side)))
                n += 1
        return late + passed

    def settle(pieces):
        for piece in pieces:
            arrived(piece)

    share = blocks * HEAD

    def share_rows(r):
        return pl.ds(mult(r * share, share), share)

    def back_early(t, own):
        @pl.loop(0, quarters)
        def _(r):
            total = dot(fm[t, 0, share_rows(r), :], flat(own, 0), 1, 1)
            for u in range(1, last):
                total = total + dot(fm[t, u, share_rows(r), :], flat(own, u), 1, 1)
            early[share_rows(r), :] = total

    def back_tail(t, own):
        total = dot(ft[t, :, :hw], flat(own, 0), 1, 1)
        for u in range(1, PARTS):
            total = total + dot(ft[t, :, u * hw : (u + 1) * hw], flat(own, u), 1, 1)
        tail32[...] = total

    def back_share(t, own, r):
        total = early[share_rows(r), :] + dot(fm[t, last, share_rows(r), :], flat(own, last), 1, 1)
        part = total.astype(BF)
        for g in range(blocks):
            back_msg[t, r, g, :HEAD, :] = part[g * HEAD : (g + 1) * HEAD, :]
            back_msg[t, r, g, HEAD:, :] = tail32[g * TAIL : (g + 1) * TAIL, :].astype(BF)

    def fold_near(t, own):
        dev = {"dp": e * quarters + near_q}
        out = []
        for i, r in ((1, near_far_q), (0, near_q)):
            back_share(t, own, r)
            out += start([remote(back_msg.at[t, r], sum_in.at[t, i], fold_send.at[t, i], fold_recv.at[t, i], dev)])
        for r in (far_q, q):
            back_share(t, own, r)
        return out

    def fold_far(t, near):
        for n, (i, r) in enumerate(((1, far_q), (0, q))):
            arrived(near[n : n + 1])
            for g in range(blocks):
                total = back_msg[t, r, g].astype(F32) + sum_in[t, i, g].astype(F32)
                back_msg[t, r, g] = total.astype(BF)
            if i == 1:
                dev = {"dp": e * quarters + far_q}
                out = start(
                    [remote(back_msg.at[t, r], sum_far.at[t], fold_send.at[t, 2], fold_recv.at[t, 2], dev)]
                )
        return out

    def give_back(t, got):
        for g in range(blocks):
            total = back_msg[t, q, g].astype(F32) + sum_far[t, g].astype(F32)
            back_msg[t, q, g] = total.astype(BF)

        @pl.loop(1, blocks)
        def _(i):
            g = lax.rem(e + i, blocks)
            remote(back_msg.at[t, q, g], got.at[e], o_send.at[t], o_recv.at[t], {"dp": g * quarters + q}).start()

        pltpu.make_async_copy(back_msg.at[t, q, e], got.at[e], o_recv.at[t]).start()

    def returned(got):
        return got[...].astype(F32).reshape(E * MSG, own_f)

    def gradient(main, tail, t, u, out):
        @pl.loop(0, hw // 128)
        def _(c):
            at = mult(c * 128, 128)
            g = dot(main[...], fm[t, u, :, pl.ds(at, 128)], 0, 0)
            g = g + dot(tail[...], ft[t, :, pl.ds(u * hw + at, 128)], 0, 0)
            out[:, pl.ds(u * hw + at, 128)] = g.astype(BF)

    send_tokens(0, x_msg, x_got)
    send_weights(0, 0, up, up_own, 0, 20)
    keep_weights(0, up, up_own)
    keep_weights(1, down, down_own)
    take(x_got.at[q], t_recv.at[0])
    xf = relay_far(0, x_got)
    send_weights(0, 0, up, up_own, 20, n_dp - 1)
    arrived(xf)
    xn = relay_near(0, x_got)
    send_weights(0, 1, up, up_own, 0, n_dp - 1)
    pt[:, :, hid:] = jnp.zeros((2, t_rows, pt.shape[2] - hid), BF)
    arrived(xn)
    gather_rows(x_got, xm, xt)

    take(up_own.at[0], w_recv.at[0])
    partial(0, 0, xm, xt, up_own)
    rs_0 = rs_begin(0, 0)
    send_tokens(1, d_msg, d_got)
    send_weights(1, 0, down, down_own, 0, n_dp - 1)
    rs_join(0, 0, rs_0)
    sum_first(0, 0)
    small_0 = rs_small(0, 0)

    take(up_own.at[1], w_recv.at[1])
    partial(0, 1, xm, xt, up_own)
    rs_1 = rs_begin(0, 1)
    take(d_got.at[q], t_recv.at[1])
    df = relay_far(1, d_got)
    arrived(small_0)
    finish(0, 0, silu)
    gather_0 = ag_small(0, 0)
    send_weights(1, 1, down, down_own, 0, n_dp - 1)
    rs_join(0, 1, rs_1)
    sum_first(0, 1)
    small_1 = rs_small(0, 1)
    arrived(gather_0)
    ag_0 = ag_big(0, 0)
    arrived(df)
    dn = relay_near(1, d_got)
    arrived(dn)
    gather_rows(d_got, dm, dt)

    take(down_own.at[0], w_recv.at[2])
    partial(1, 0, dm, dt, down_own)
    rs_2 = rs_begin(1, 0)
    arrived(small_1)
    finish(0, 1, silu)
    gather_1 = ag_small(0, 1)
    rest_0 = ag_pass(0, 0, ag_0)
    rs_join(1, 0, rs_2)
    sum_first(1, 0)
    small_2 = rs_small(1, 0)
    arrived(gather_1)
    ag_1 = ag_big(0, 1)

    take(down_own.at[1], w_recv.at[3])
    partial(1, 1, dm, dt, down_own)
    before_3 = len(started)
    rs_3 = rs_begin(1, 1)
    arrived(small_2)
    finish(1, 0, silu_back)
    gather_2 = ag_small(1, 0)
    rest_1 = ag_pass(0, 1, ag_1)
    settle(rest_0)
    rs_join(1, 1, rs_3)
    sum_first(1, 1)
    small_3 = rs_small(1, 1)
    arrived(gather_2)
    ag_2 = ag_big(1, 0)
    back_early(0, down_own)
    settle(rest_1)
    back_tail(0, down_own)
    near_0 = fold_near(0, down_own)
    arrived(small_3)
    finish(1, 1, silu_back)
    gather_3 = ag_small(1, 1)
    rest_2 = ag_pass(1, 0, ag_2)
    far_0 = fold_far(0, near_0)
    drain(before_3)
    arrived(gather_3)
    ag_3 = ag_big(1, 1)
    arrived(far_0)
    give_back(0, y_got)
    rest_3 = ag_pass(1, 1, ag_3)
    settle(rest_2)
    back_early(1, up_own)
    gradient(dm, dt, 0, 0, gd_out)
    gradient(dm, dt, 0, 1, gd_out)
    settle(rest_3)
    back_tail(1, up_own)
    near_1 = fold_near(1, up_own)
    far_1 = fold_far(1, near_1)
    arrived(far_1)
    give_back(1, dx_got)
    gradient(xm, xt, 1, 0, gu_out)
    gradient(xm, xt, 1, 1, gu_out)
    take(y_got, o_recv.at[0])
    mixed_out[...] = lax.dot_general(
        weighted[...], returned(y_got), (((0,), (0,)), ((), ())),
        precision=lax.Precision.HIGHEST, preferred_element_type=F32,
    ).astype(BF)
    drain(len(started))
    for t, own in enumerate((up_own, down_own)):
        for u in range(PARTS):
            take(own.at[u, pl.ds(0, n_dp - 1)], w_send.at[t * PARTS + u])
    for n, got in enumerate((x_got, d_got)):
        take(got.at[0, pl.ds(0, blocks - 1)], t_send.at[n])
    take(dx_got, o_recv.at[1])
    gt_out[...] = dot(pick[...], returned(dx_got).astype(BF), 0, 0).astype(BF)
    for n, got in enumerate((y_got, dx_got)):
        take(got.at[pl.ds(0, blocks - 1)], o_send.at[n])


def layer(x_msg, d_msg, weighted, pick, up, down):
    n_dp = lax.axis_size("dp")
    own_f = x_msg.shape[2]
    rows = up.shape[1]
    quarters = n_dp // E
    blocks = n_dp // quarters
    hid = up.shape[2] // quarters
    hw = hid // PARTS
    main = n_dp * HEAD
    tails = blocks * TAIL
    wide = -(-hid // (SIDE * SIDE * 128)) * SIDE * SIDE * 128
    big = main // 2 // SIDE
    small = big // SIDE
    ht = tails // 2
    vm = pltpu.VMEM
    dma = pltpu.SemaphoreType.DMA
    return pl.pallas_call(
        layer_kernel,
        name="layer",
        out_shape=(
            jax.ShapeDtypeStruct((weighted.shape[1], own_f), BF),
            jax.ShapeDtypeStruct((weighted.shape[1], own_f), BF),
            jax.ShapeDtypeStruct((own_f, hid), BF),
            jax.ShapeDtypeStruct((own_f, hid), BF),
        ),
        in_specs=[pl.BlockSpec(memory_space=pltpu.VMEM)] * 4 + [pl.BlockSpec(memory_space=pl.ANY)] * 2,
        out_specs=[pl.BlockSpec(memory_space=pltpu.VMEM)] * 4,
        scratch_shapes=[
            vm((E, MSG, own_f), BF), vm((E, MSG, own_f), BF),
            vm((PARTS, n_dp, rows, hw), BF), vm((PARTS, n_dp, rows, hw), BF),
            vm((quarters, blocks, MSG, own_f), BF), vm((quarters, blocks, MSG, own_f), BF),
            vm((2, quarters, blocks, MSG, own_f), BF), vm((2, 2, blocks, MSG, own_f), BF),
            vm((2, blocks, MSG, own_f), BF),
            vm((main, own_f), BF), vm((tails, own_f), BF),
            vm((main, own_f), BF), vm((tails, own_f), BF),
            vm((tails, own_f), F32), vm((main, own_f), F32),
            vm((2, PARTS, main, hw), BF), vm((2, tails, wide), BF),
            vm((2, PARTS, 2, 2, big // 2, hw), BF), vm((2, 2, 2, ht // 2, wide // SIDE), BF),
            vm((2, PARTS, 2, 2, 2, big // 2, hw), BF), vm((2, 2, 2, 2, ht // 2, wide // SIDE), BF),
            vm((2, PARTS, 2, big, hw), BF), vm((2, 2, ht, wide // SIDE), BF),
            vm((2, PARTS, 2, SIDE - 1, small, hw), BF), vm((2, 2, SIDE - 1, ht, wide // SIDE // SIDE), BF),
            vm((PARTS, 2, small, hw), F32), vm((2, ht, wide // SIDE // SIDE), F32),
            vm((2, PARTS, main, hw), BF), vm((2, tails, wide), BF),
            dma((2 * PARTS,)), dma((2 * PARTS,)), dma((2,)), dma((2,)),
            dma((2, 3)), dma((2, 3)), dma((2, 3)), dma((2, 3)), dma((2,)), dma((2,)),
            dma((2 * PARTS, 2, 6, 2)), dma((2 * PARTS, 2, 6, 2)),
            dma((2 * PARTS, 2, SIDE - 1, 2)), dma((2 * PARTS, 2, SIDE - 1, 2)),
            dma((2 * PARTS, 2, SIDE - 1, 2)), dma((2 * PARTS, 2, SIDE - 1, 2)),
            dma((2 * PARTS, 2, 6, 2)), dma((2 * PARTS, 2, 6, 2)),
        ],
        compiler_params=pltpu.CompilerParams(
            collective_id=0, has_side_effects=True, vmem_limit_bytes=58 * 2**20
        ),
    )(x_msg, d_msg, weighted, pick, up, down)


def body(tokens, routes, route_weights, up_stacked, down_stacked, cotangent):
    experts = jnp.arange(E, dtype=jnp.int32)
    named = routes[:, :, None] == experts[None, None, :]
    chosen = jnp.sum(named.astype(F32), axis=1)
    rows = jnp.arange(routes.shape[0], dtype=jnp.int32)
    earlier = (rows[None, :] < rows[:, None]).astype(BF)
    before = jnp.dot(earlier, chosen.astype(BF), preferred_element_type=F32).astype(jnp.int32)
    slot_pos = jnp.sum(jnp.where(named, before[:, None, :], 0), axis=2)
    shift = 2 * lax.rem(lax.axis_index("dp"), 4)
    target = routes * MSG + slot_pos + jnp.where(slot_pos >= HEAD, shift, 0)
    slot_hits = jnp.arange(E * MSG, dtype=jnp.int32)[:, None, None] == target[None, :, :]
    pick_table = jnp.sum(slot_hits.astype(F32), axis=2)
    weighted = jnp.sum(jnp.where(slot_hits, route_weights[None, :, :], 0.0), axis=2)
    features = tokens.shape[1]
    x_msg = jnp.dot(pick_table.astype(BF), tokens, preferred_element_type=F32).astype(BF)
    d_msg = jnp.dot(weighted, cotangent.astype(F32), precision=lax.Precision.HIGHEST).astype(BF)
    mixed, grad_tokens, g_up, g_down = layer(
        x_msg.reshape(E, MSG, features), d_msg.reshape(E, MSG, features), weighted, pick_table.astype(BF),
        up_stacked, down_stacked,
    )
    return (mixed, grad_tokens, g_up[None], g_down[None])


def solution(mesh):
    placed = (
        P("dp", "member"),
        P("dp", None),
        P("dp", None),
        P(None, ("member", "dp"), None),
        P(None, ("member", "dp"), None),
        P("dp", "member"),
    )
    return jax.shard_map(
        body,
        mesh=mesh,
        in_specs=placed,
        out_specs=(
            P("dp", "member"),
            P("dp", "member"),
            P("dp", "member", None),
            P("dp", "member", None),
        ),
        check_vma=False,
    )
```

```python
import jax
import jax.numpy as jnp
from jax import lax
from jax.experimental import pallas as pl
from jax.experimental.pallas import tpu as pltpu
from jax.sharding import PartitionSpec as P

FF_W = 7168
E = 8
CAP = 34
SIDE = 4
PARTS = 2
HEAD = 32
TAIL = 8
MSG = HEAD + TAIL
BF = jnp.bfloat16
F32 = jnp.float32


def dot(a, b, ca, cb):
    return lax.dot_general(a, b, (((ca,), (cb,)), ((), ())), preferred_element_type=F32)


def mult(i, n):
    return pl.multiple_of(i, n)


def layer_kernel(
    tokens, cotangent, weighted, pick, up, down,
    mixed_out, gt_out, gu_out, gd_out,
    x_msg, d_msg, y_got, dx_got,
    up_own, down_own, x_got, d_got, back_msg, sum_in, sum_far,
    xm, xt, dm, dt, tail32, early,
    pm, pt, ram, rat, rbm, rbt, sm, st, r2m, r2t, pre_m, pre_t, fm, ft,
    w_send, w_recv, t_send, t_recv, relay_send, relay_recv, fold_send, fold_recv, o_send, o_recv,
    rs_send, rs_recv, rs2_send, rs2_recv, ag_send, ag_recv, ag2_send, ag2_recv,
):
    n_dp = lax.axis_size("dp")
    quarters = n_dp // E
    blocks = n_dp // quarters
    hw = up_own.shape[3]
    hid = PARTS * hw
    last = PARTS - 1
    own_f = xm.shape[1]
    j = lax.axis_index("dp")
    m = lax.axis_index("member")
    e, q = j // quarters, lax.rem(j, quarters)
    far_q = lax.rem(q + 2, 4)
    near_q = q + 1 - 2 * lax.rem(q, 2)
    near_far_q = lax.rem(near_q + 2, 4)
    cy, cx = m // SIDE, lax.rem(m, SIDE)
    half_rows = n_dp * HEAD // 2
    big = half_rows // SIDE
    small = big // SIDE
    t_rows = blocks * TAIL
    ht = t_rows // 2
    wide = pt.shape[2] // SIDE
    narrow = wide // SIDE
    started = []

    def first(h):
        return cx if h == 0 else cy

    def second(h):
        return cy if h == 0 else cx

    def peer_first(h, k):
        c = lax.rem(first(h) + k, SIDE)
        return c, {"member": cy * SIDE + c if h == 0 else c * SIDE + cx}

    def peer_second(h, k):
        c = lax.rem(second(h) + k, SIDE)
        return c, {"member": c * SIDE + cx if h == 0 else cy * SIDE + c}

    def shifted(i):
        step = i // 2 + 1
        return lax.rem(j + n_dp + step * (1 - 2 * lax.rem(i, 2)), n_dp)

    barrier = pltpu.get_barrier_semaphore()

    @pl.loop(0, n_dp - 1)
    def _(i):
        pl.semaphore_signal(barrier, inc=1, device_id={"dp": shifted(i)})

    for k in range(1, SIDE):
        pl.semaphore_signal(barrier, inc=1, device_id=peer_first(0, k)[1])
        pl.semaphore_signal(barrier, inc=1, device_id=peer_first(1, k)[1])
    rows = dot(pick[...], tokens[...], 1, 0)
    x_msg[...] = rows.reshape(E, MSG, own_f).astype(BF)
    rows = lax.dot_general(
        weighted[...], cotangent[...].astype(F32), (((1,), (0,)), ((), ())),
        precision=lax.Precision.HIGHEST, preferred_element_type=F32,
    )
    d_msg[...] = rows.reshape(E, MSG, own_f).astype(BF)
    pl.semaphore_wait(barrier, n_dp - 1 + 2 * (SIDE - 1))

    def remote(src, dst, send, recv, dev):
        return pltpu.make_async_remote_copy(
            src_ref=src, dst_ref=dst, send_sem=send, recv_sem=recv, device_id=dev
        )

    def start(copies):
        for c in copies:
            c.start()
        started.extend(copies)
        return copies

    def drain(count):
        for c in started[:count]:
            c.wait_send()
        del started[:count]

    def arrived(copies):
        for c in copies:
            c.wait_recv()

    def take(buf, sem):
        pltpu.make_async_copy(buf, buf, sem).wait()

    def weight_part(w, u, who):
        column = lax.rem(who, quarters) * hid + u * hw
        return w.at[who // quarters, :, pl.ds(mult(column, 128), hw)]

    def send_weights(t, u, w, own, lo, hi):
        n = t * PARTS + u

        @pl.loop(lo, hi)
        def _(i):
            who = shifted(i)
            remote(weight_part(w, u, who), own.at[u, j], w_send.at[n], w_recv.at[n], {"dp": who}).start()

    def keep_weights(t, w, own):
        for u in range(PARTS):
            pltpu.make_async_copy(weight_part(w, u, j), own.at[u, j], w_recv.at[t * PARTS + u]).start()

    def send_tokens(n, msg, got):
        @pl.loop(1, blocks)
        def _(i):
            g = lax.rem(e + i, blocks)
            remote(msg.at[g], got.at[q, e], t_send.at[n], t_recv.at[n], {"dp": g * quarters + q}).start()

        pltpu.make_async_copy(msg.at[e], got.at[q, e], t_recv.at[n]).start()

    def relay_far(n, got):
        dev = {"dp": e * quarters + far_q}
        return start([remote(got.at[q], got.at[q], relay_send.at[n, 0], relay_recv.at[n, 0], dev)])

    def relay_near(n, got):
        dev = {"dp": e * quarters + near_q}
        return start(
            [
                remote(got.at[r], got.at[r], relay_send.at[n, 1 + i], relay_recv.at[n, 1 + i], dev)
                for i, r in enumerate((q, far_q))
            ]
        )

    def gather_rows(got, main, tail):
        @pl.loop(0, quarters)
        def _(r):
            for g in range(blocks):
                main[pl.ds(mult((r * blocks + g) * HEAD, HEAD), HEAD), :] = got[r, g, :HEAD, :]

        @pl.loop(0, blocks)
        def _(g):
            total = got[0, g, HEAD:, :].astype(F32)
            for r in range(1, quarters):
                total = total + got[r, g, HEAD:, :].astype(F32)
            tail32[pl.ds(mult(g * TAIL, TAIL), TAIL), :] = total

        tail[...] = tail32[...].astype(BF)

    def flat(own, u):
        return own[u].reshape(own_f, hw)

    def partial(t, u, main, tail, own):
        rows = n_dp * HEAD // 4

        @pl.loop(0, 4)
        def _(i):
            block = pl.ds(mult(i * rows, rows), rows)
            pm[t, u, block, :] = dot(main[block, :], flat(own, u), 1, 0).astype(BF)

        if u == last:
            for v in range(PARTS):
                pt[t, :, v * hw : (v + 1) * hw] = dot(tail[...], flat(own, v), 1, 0).astype(BF)

    RIGHT, LEFT, FACING = 1, 3, 2
    hb, htb = big // 2, ht // 2

    def chunk_main(h, c, part):
        return pl.ds(mult(h * half_rows + c * big + part * hb, hb), hb)

    def chunk_tail(h, c, part):
        return pl.ds(h * ht + part * htb, htb), pl.ds(mult(c * wide, wide), wide)

    def rs_piece(t, u, h, to, c, part, dst_m, dst_t, n):
        dev = peer_first(h, to)[1]
        p = t * PARTS + u
        src = pm.at[t, u, chunk_main(h, c, part), :]
        out = [remote(src, dst_m, rs_send.at[p, h, n, 0], rs_recv.at[p, h, n, 0], dev)]
        if u == last:
            rows, cols = chunk_tail(h, c, part)
            out.append(remote(pt.at[t, rows, cols], dst_t, rs_send.at[p, h, n, 1], rs_recv.at[p, h, n, 1], dev))
        return out

    def rs_begin(t, u):
        passing, direct, joined = [], [], []
        for h in range(2):
            for side, to in enumerate((RIGHT, LEFT)):
                facing = peer_first(h, FACING)[0]
                c = peer_first(h, to)[0]
                a, b = (ram.at[t, u, h, side], rat.at[t, h, side]), (rbm.at[t, u, h, side], rbt.at[t, h, side])
                passing.append(rs_piece(t, u, h, to, facing, side, *a, side))
                direct.append(rs_piece(t, u, h, to, c, 1 - side, b[0].at[1 - side], b[1].at[1 - side], 2 + side))
                joined.append(rs_piece(t, u, h, to, c, side, b[0].at[side], b[1].at[side], 4 + side))
        for piece in passing + direct:
            start(piece)
        return passing, direct, joined

    def rs_join(t, u, pieces):
        passing, direct, joined = pieces
        n = 0
        for h in range(2):
            for side, to in enumerate((RIGHT, LEFT)):
                arrived(passing[n])
                c = peer_first(h, to)[0]
                base = h * half_rows + c * big + side * hb

                @pl.loop(0, hb // 16)
                def _(i):
                    rows = pl.ds(mult(base + i * 16, 16), 16)
                    got = ram[t, u, h, side, pl.ds(mult(i * 16, 16), 16), :]
                    pm[t, u, rows, :] = (pm[t, u, rows, :].astype(F32) + got.astype(F32)).astype(BF)

                if u == last:
                    rows, cols = chunk_tail(h, c, side)
                    pt[t, rows, cols] = (pt[t, rows, cols].astype(F32) + rat[t, h, side].astype(F32)).astype(BF)
                start(joined[n])
                n += 1
        for piece in direct + joined:
            arrived(piece)

    def sum_first(t, u):
        for h in range(2):
            for part in range(2):
                base = h * half_rows + first(h) * big + part * hb

                @pl.loop(0, hb // 16)
                def _(i):
                    rows = pl.ds(mult(i * 16, 16), 16)
                    total = pm[t, u, pl.ds(mult(base + i * 16, 16), 16), :].astype(F32)
                    for side in range(2):
                        total = total + rbm[t, u, h, side, part, rows, :].astype(F32)
                    sm[t, u, h, pl.ds(mult(part * hb + i * 16, 16), 16), :] = total.astype(BF)

                if u == last:
                    rows, cols = chunk_tail(h, first(h), part)
                    total = pt[t, rows, cols].astype(F32)
                    for side in range(2):
                        total = total + rbt[t, h, side, part].astype(F32)
                    st[t, h, part * htb : (part + 1) * htb, :] = total.astype(BF)

    def rs_small(t, u):
        out = []
        p = t * PARTS + u
        for h in range(2):
            for k in range(1, SIDE):
                c, dev = peer_second(h, k)
                pairs = [(sm.at[t, u, h, pl.ds(mult(c * small, small), small), :], r2m.at[t, u, h, k - 1])]
                if u == last:
                    pairs.append((st.at[t, h, :, pl.ds(mult(c * narrow, narrow), narrow)], r2t.at[t, h, k - 1]))
                for n, (src, dst) in enumerate(pairs):
                    out.append(remote(src, dst, rs2_send.at[p, h, k - 1, n], rs2_recv.at[p, h, k - 1, n], dev))
        return start(out)

    def owned_rows(h):
        return pl.ds(mult(h * half_rows + first(h) * big + second(h) * small, small), small)

    def owned_cols(h):
        return pl.ds(mult(first(h) * wide + second(h) * narrow, narrow), narrow)

    def finish(t, u, fn):
        for h in range(2):

            @pl.loop(0, small // 16)
            def _(i):
                rows = pl.ds(mult(i * 16, 16), 16)
                total = sm[t, u, h, pl.ds(mult(second(h) * small + i * 16, 16), 16), :].astype(F32)
                for k in range(SIDE - 1):
                    total = total + r2m[t, u, h, k, rows, :].astype(F32)
                start_row = h * half_rows + first(h) * big + second(h) * small
                fm[t, u, pl.ds(mult(start_row + i * 16, 16), 16), :] = fn(total, pre_m.at[u, h, rows, :]).astype(BF)

            if u == last:
                total = st[t, h, :, pl.ds(mult(second(h) * narrow, narrow), narrow)].astype(F32)
                for k in range(SIDE - 1):
                    total = total + r2t[t, h, k].astype(F32)
                ft[t, pl.ds(h * ht, ht), owned_cols(h)] = fn(total, pre_t.at[h]).astype(BF)

    def silu(total, keep):
        keep[...] = total
        return total / (1.0 + jnp.exp(-total))

    def silu_back(total, keep):
        pre = keep[...]
        s = 1.0 / (1.0 + jnp.exp(-pre))
        return total * s * (1.0 + pre * (1.0 - s))

    def ag_small(t, u):
        out = []
        p = t * PARTS + u
        for h in range(2):
            for k in range(1, SIDE):
                dev = peer_second(h, k)[1]
                refs = [fm.at[t, u, owned_rows(h), :]]
                if u == last:
                    refs.append(ft.at[t, pl.ds(h * ht, ht), owned_cols(h)])
                for n, ref in enumerate(refs):
                    out.append(remote(ref, ref, ag_send.at[p, h, k - 1, n], ag_recv.at[p, h, k - 1, n], dev))
        return start(out)

    def ag_piece(t, u, h, to, c, part, n):
        dev = peer_first(h, to)[1]
        p = t * PARTS + u
        refs = [fm.at[t, u, chunk_main(h, c, part), :]]
        if u == last:
            rows, cols = chunk_tail(h, c, part)
            refs.append(ft.at[t, rows, cols])
        return [
            remote(ref, ref, ag2_send.at[p, h, n, i], ag2_recv.at[p, h, n, i], dev) for i, ref in enumerate(refs)
        ]

    def ag_big(t, u):
        soon, late = [], []
        for h in range(2):
            for side, to in enumerate((RIGHT, LEFT)):
                soon.append(start(ag_piece(t, u, h, to, first(h), side, side)))
        for h in range(2):
            for side, to in enumerate((RIGHT, LEFT)):
                late.append(start(ag_piece(t, u, h, to, first(h), 1 - side, 2 + side)))
        return soon, late

    def ag_pass(t, u, pieces):
        soon, late = pieces
        passed = []
        n = 0
        for h in range(2):
            for side, to in enumerate((RIGHT, LEFT)):
                arrived(soon[n])
                back_c = peer_first(h, LEFT if to == RIGHT else RIGHT)[0]
                passed.append(start(ag_piece(t, u, h, to, back_c, side, 4 + side)))
                n += 1
        return late + passed

    def settle(pieces):
        for piece in pieces:
            arrived(piece)

    share = blocks * HEAD

    def share_rows(r):
        return pl.ds(mult(r * share, share), share)

    def back_early(t, own):
        @pl.loop(0, quarters)
        def _(r):
            total = dot(fm[t, 0, share_rows(r), :], flat(own, 0), 1, 1)
            for u in range(1, last):
                total = total + dot(fm[t, u, share_rows(r), :], flat(own, u), 1, 1)
            early[share_rows(r), :] = total

    def back_tail(t, own):
        total = dot(ft[t, :, :hw], flat(own, 0), 1, 1)
        for u in range(1, PARTS):
            total = total + dot(ft[t, :, u * hw : (u + 1) * hw], flat(own, u), 1, 1)
        tail32[...] = total

    def back_share(t, own, r):
        total = early[share_rows(r), :] + dot(fm[t, last, share_rows(r), :], flat(own, last), 1, 1)
        part = total.astype(BF)
        for g in range(blocks):
            back_msg[t, r, g, :HEAD, :] = part[g * HEAD : (g + 1) * HEAD, :]
            back_msg[t, r, g, HEAD:, :] = tail32[g * TAIL : (g + 1) * TAIL, :].astype(BF)

    def fold_near(t, own):
        dev = {"dp": e * quarters + near_q}
        out = []
        for i, r in ((1, near_far_q), (0, near_q)):
            back_share(t, own, r)
            out += start([remote(back_msg.at[t, r], sum_in.at[t, i], fold_send.at[t, i], fold_recv.at[t, i], dev)])
        for r in (far_q, q):
            back_share(t, own, r)
        return out

    def fold_far(t, near):
        for n, (i, r) in enumerate(((1, far_q), (0, q))):
            arrived(near[n : n + 1])
            for g in range(blocks):
                total = back_msg[t, r, g].astype(F32) + sum_in[t, i, g].astype(F32)
                back_msg[t, r, g] = total.astype(BF)
            if i == 1:
                dev = {"dp": e * quarters + far_q}
                out = start(
                    [remote(back_msg.at[t, r], sum_far.at[t], fold_send.at[t, 2], fold_recv.at[t, 2], dev)]
                )
        return out

    def give_back(t, got):
        for g in range(blocks):
            total = back_msg[t, q, g].astype(F32) + sum_far[t, g].astype(F32)
            back_msg[t, q, g] = total.astype(BF)

        @pl.loop(1, blocks)
        def _(i):
            g = lax.rem(e + i, blocks)
            remote(back_msg.at[t, q, g], got.at[e], o_send.at[t], o_recv.at[t], {"dp": g * quarters + q}).start()

        pltpu.make_async_copy(back_msg.at[t, q, e], got.at[e], o_recv.at[t]).start()

    def returned(got):
        return got[...].astype(F32).reshape(E * MSG, own_f)

    def gradient(main, tail, t, u, out):
        @pl.loop(0, hw // 128)
        def _(c):
            at = mult(c * 128, 128)
            g = dot(main[...], fm[t, u, :, pl.ds(at, 128)], 0, 0)
            g = g + dot(tail[...], ft[t, :, pl.ds(u * hw + at, 128)], 0, 0)
            out[:, pl.ds(u * hw + at, 128)] = g.astype(BF)

    send_tokens(0, x_msg, x_got)
    send_weights(0, 0, up, up_own, 0, 20)
    keep_weights(0, up, up_own)
    keep_weights(1, down, down_own)
    take(x_got.at[q], t_recv.at[0])
    xf = relay_far(0, x_got)
    send_weights(0, 0, up, up_own, 20, n_dp - 1)
    arrived(xf)
    xn = relay_near(0, x_got)
    send_weights(0, 1, up, up_own, 0, n_dp - 1)
    pt[:, :, hid:] = jnp.zeros((2, t_rows, pt.shape[2] - hid), BF)
    arrived(xn)
    gather_rows(x_got, xm, xt)

    take(up_own.at[0], w_recv.at[0])
    partial(0, 0, xm, xt, up_own)
    rs_0 = rs_begin(0, 0)
    send_tokens(1, d_msg, d_got)
    send_weights(1, 0, down, down_own, 0, n_dp - 1)
    rs_join(0, 0, rs_0)
    sum_first(0, 0)
    small_0 = rs_small(0, 0)

    take(up_own.at[1], w_recv.at[1])
    partial(0, 1, xm, xt, up_own)
    rs_1 = rs_begin(0, 1)
    take(d_got.at[q], t_recv.at[1])
    df = relay_far(1, d_got)
    arrived(small_0)
    finish(0, 0, silu)
    gather_0 = ag_small(0, 0)
    send_weights(1, 1, down, down_own, 0, n_dp - 1)
    rs_join(0, 1, rs_1)
    sum_first(0, 1)
    small_1 = rs_small(0, 1)
    arrived(gather_0)
    ag_0 = ag_big(0, 0)
    arrived(df)
    dn = relay_near(1, d_got)
    arrived(dn)
    gather_rows(d_got, dm, dt)

    take(down_own.at[0], w_recv.at[2])
    partial(1, 0, dm, dt, down_own)
    before_2 = len(started)
    rs_2 = rs_begin(1, 0)
    arrived(small_1)
    finish(0, 1, silu)
    gather_1 = ag_small(0, 1)
    rest_0 = ag_pass(0, 0, ag_0)
    rs_join(1, 0, rs_2)
    sum_first(1, 0)
    small_2 = rs_small(1, 0)
    arrived(gather_1)
    ag_1 = ag_big(0, 1)

    take(down_own.at[1], w_recv.at[3])
    partial(1, 1, dm, dt, down_own)
    before_3 = len(started)
    rs_3 = rs_begin(1, 1)
    arrived(small_2)
    finish(1, 0, silu_back)
    gather_2 = ag_small(1, 0)
    rest_1 = ag_pass(0, 1, ag_1)
    settle(rest_0)
    rs_join(1, 1, rs_3)
    sum_first(1, 1)
    small_3 = rs_small(1, 1)
    arrived(gather_2)
    ag_2 = ag_big(1, 0)
    back_early(0, down_own)
    settle(rest_1)
    back_tail(0, down_own)
    near_0 = fold_near(0, down_own)
    arrived(small_3)
    finish(1, 1, silu_back)
    gather_3 = ag_small(1, 1)
    rest_2 = ag_pass(1, 0, ag_2)
    far_0 = fold_far(0, near_0)
    drain(before_2)
    arrived(gather_3)
    ag_3 = ag_big(1, 1)
    arrived(far_0)
    give_back(0, y_got)
    rest_3 = ag_pass(1, 1, ag_3)
    settle(rest_2)
    back_early(1, up_own)
    gradient(dm, dt, 0, 0, gd_out)
    drain(before_3 - before_2)
    settle(rest_3)
    back_tail(1, up_own)
    near_1 = fold_near(1, up_own)
    far_1 = fold_far(1, near_1)
    arrived(far_1)
    give_back(1, dx_got)
    gradient(dm, dt, 0, 1, gd_out)
    gradient(xm, xt, 1, 0, gu_out)
    gradient(xm, xt, 1, 1, gu_out)
    take(y_got, o_recv.at[0])
    mixed_out[...] = lax.dot_general(
        weighted[...], returned(y_got), (((0,), (0,)), ((), ())),
        precision=lax.Precision.HIGHEST, preferred_element_type=F32,
    ).astype(BF)
    drain(len(started))
    for t, own in enumerate((up_own, down_own)):
        for u in range(PARTS):
            take(own.at[u, pl.ds(0, n_dp - 1)], w_send.at[t * PARTS + u])
    for n, got in enumerate((x_got, d_got)):
        take(got.at[0, pl.ds(0, blocks - 1)], t_send.at[n])
    take(dx_got, o_recv.at[1])
    gt_out[...] = dot(pick[...], returned(dx_got).astype(BF), 0, 0).astype(BF)
    for n, got in enumerate((y_got, dx_got)):
        take(got.at[pl.ds(0, blocks - 1)], o_send.at[n])


def layer(tokens, cotangent, weighted, pick, up, down):
    n_dp = lax.axis_size("dp")
    own_f = tokens.shape[1]
    rows = up.shape[1]
    quarters = n_dp // E
    blocks = n_dp // quarters
    hid = up.shape[2] // quarters
    hw = hid // PARTS
    main = n_dp * HEAD
    tails = blocks * TAIL
    wide = -(-hid // (SIDE * SIDE * 128)) * SIDE * SIDE * 128
    big = main // 2 // SIDE
    small = big // SIDE
    ht = tails // 2
    vm = pltpu.VMEM
    dma = pltpu.SemaphoreType.DMA
    return pl.pallas_call(
        layer_kernel,
        name="layer",
        out_shape=(
            jax.ShapeDtypeStruct((weighted.shape[1], own_f), BF),
            jax.ShapeDtypeStruct((weighted.shape[1], own_f), BF),
            jax.ShapeDtypeStruct((own_f, hid), BF),
            jax.ShapeDtypeStruct((own_f, hid), BF),
        ),
        in_specs=[pl.BlockSpec(memory_space=pltpu.VMEM)] * 4 + [pl.BlockSpec(memory_space=pl.ANY)] * 2,
        out_specs=[pl.BlockSpec(memory_space=pltpu.VMEM)] * 4,
        scratch_shapes=[
            vm((E, MSG, own_f), BF), vm((E, MSG, own_f), BF),
            vm((E, MSG, own_f), BF), vm((E, MSG, own_f), BF),
            vm((PARTS, n_dp, rows, hw), BF), vm((PARTS, n_dp, rows, hw), BF),
            vm((quarters, blocks, MSG, own_f), BF), vm((quarters, blocks, MSG, own_f), BF),
            vm((2, quarters, blocks, MSG, own_f), BF), vm((2, 2, blocks, MSG, own_f), BF),
            vm((2, blocks, MSG, own_f), BF),
            vm((main, own_f), BF), vm((tails, own_f), BF),
            vm((main, own_f), BF), vm((tails, own_f), BF),
            vm((tails, own_f), F32), vm((main, own_f), F32),
            vm((2, PARTS, main, hw), BF), vm((2, tails, wide), BF),
            vm((2, PARTS, 2, 2, big // 2, hw), BF), vm((2, 2, 2, ht // 2, wide // SIDE), BF),
            vm((2, PARTS, 2, 2, 2, big // 2, hw), BF), vm((2, 2, 2, 2, ht // 2, wide // SIDE), BF),
            vm((2, PARTS, 2, big, hw), BF), vm((2, 2, ht, wide // SIDE), BF),
            vm((2, PARTS, 2, SIDE - 1, small, hw), BF), vm((2, 2, SIDE - 1, ht, wide // SIDE // SIDE), BF),
            vm((PARTS, 2, small, hw), F32), vm((2, ht, wide // SIDE // SIDE), F32),
            vm((2, PARTS, main, hw), BF), vm((2, tails, wide), BF),
            dma((2 * PARTS,)), dma((2 * PARTS,)), dma((2,)), dma((2,)),
            dma((2, 3)), dma((2, 3)), dma((2, 3)), dma((2, 3)), dma((2,)), dma((2,)),
            dma((2 * PARTS, 2, 6, 2)), dma((2 * PARTS, 2, 6, 2)),
            dma((2 * PARTS, 2, SIDE - 1, 2)), dma((2 * PARTS, 2, SIDE - 1, 2)),
            dma((2 * PARTS, 2, SIDE - 1, 2)), dma((2 * PARTS, 2, SIDE - 1, 2)),
            dma((2 * PARTS, 2, 6, 2)), dma((2 * PARTS, 2, 6, 2)),
        ],
        compiler_params=pltpu.CompilerParams(
            collective_id=0, has_side_effects=True, vmem_limit_bytes=58 * 2**20
        ),
    )(tokens, cotangent, weighted, pick, up, down)


def body(tokens, routes, route_weights, up_stacked, down_stacked, cotangent):
    experts = jnp.arange(E, dtype=jnp.int32)
    named = routes[:, :, None] == experts[None, None, :]
    chosen = jnp.sum(named.astype(F32), axis=1)
    rows = jnp.arange(routes.shape[0], dtype=jnp.int32)
    earlier = (rows[None, :] < rows[:, None]).astype(BF)
    before = jnp.dot(earlier, chosen.astype(BF), preferred_element_type=F32).astype(jnp.int32)
    slot_pos = jnp.sum(jnp.where(named, before[:, None, :], 0), axis=2)
    shift = 2 * lax.rem(lax.axis_index("dp"), 4)
    target = routes * MSG + slot_pos + jnp.where(slot_pos >= HEAD, shift, 0)
    slot_hits = jnp.arange(E * MSG, dtype=jnp.int32)[:, None, None] == target[None, :, :]
    pick_table = jnp.sum(slot_hits.astype(F32), axis=2)
    weighted = jnp.sum(jnp.where(slot_hits, route_weights[None, :, :], 0.0), axis=2)
    mixed, grad_tokens, g_up, g_down = layer(
        tokens, cotangent, weighted, pick_table.astype(BF), up_stacked, down_stacked
    )
    return (mixed, grad_tokens, g_up[None], g_down[None])


def solution(mesh):
    placed = (
        P("dp", "member"),
        P("dp", None),
        P("dp", None),
        P(None, ("member", "dp"), None),
        P(None, ("member", "dp"), None),
        P("dp", "member"),
    )
    return jax.shard_map(
        body,
        mesh=mesh,
        in_specs=placed,
        out_specs=(
            P("dp", "member"),
            P("dp", "member"),
            P("dp", "member", None),
            P("dp", "member", None),
        ),
        check_vma=False,
    )
```
